32 devices in a mesh: grp: 2 (over x), seq: 8 (over z, y), ten: 2 (over core).
Axes of the slice: x: 2, y: 2, z: 4, core: 2. Of those that a mesh axis runs over, the one named last changes fastest.
Arguments:
- queries: bfloat16 [1024, 4096], P(('grp', 'seq'), 'ten'), parts along dimension 0, may hold values from -128 to 128
- keys: bfloat16 [1024, 512], P(('grp', 'seq'), 'ten'), parts along dimension 0, may hold values from -6 to 6
- values: bfloat16 [1024, 512], P(('grp', 'seq'), 'ten'), parts along dimension 0, may hold values from -6 to 6
- hidden: bfloat16 [1024, 8192], P(('grp', 'seq')), parts along dimension 0, may hold values from -6 to 6
- norm_gain: float32 [8192], replicated, may hold values from 0.1 to 1.9
- retained_lists: int32 [1024], P(('grp', 'seq')), parts along dimension 0, may hold values from -1 to 63, as said below
- counts: int32 [16], P('grp'), parts along dimension 0, may hold values from 0 to 64, as said below
- affine_matrix: bfloat16 [8192, 5120], P('seq', 'ten'), may hold values from -0.0625 to 0.0625
- affine_offset_vector: float32 [5120], P('ten'), may hold values from -3 to 3
Outputs:
- context: float32 [1024, 4096], P(('grp', 'seq'), 'ten'), parts along dimension 0
- col_scores: float32 [1024], P(('grp', 'seq')), parts along dimension 0
- tier_third_mapped_triples: float32 [512, 5120], P(('grp', 'seq'), 'ten'), parts along dimension 0
The draws below stay inside these ranges and needn't reach their ends.
There are 2 independent parts, one for each index of `grp`. The reference program is written for one: setup_inputs(seed, part) draws one part's arguments, and reference() takes and returns one part's arrays. A program takes and returns all parts, laid end to end along the dimension named above; an argument that names none is the same for every part. Nothing has to cross between parts.
Inputs may be any that keep to these rules, and one draw needn't show every extreme that they name: `retained_lists`: entries s*64 to (s+1)*64 - 1 hold, in their first counts[s] places, the kept local rows of shard s in rising order, and -1 after them. counts sum to 256; some shard keeps all its 64 rows.
All inputs are finite; a program needn't handle non-finite values.
Results may differ from the reference program's by a relative error of at most 0.0027.
Values may be sent and summed in bfloat16 or wider, within the bound.
A program may use at most 64 MiB of HBM per device.

```python
import math
import jax
import jax.numpy as jnp
from jax import lax

D = 8192
HEAD_SIZE = 128
QUERY_HEADS = 32
KEY_VALUE_HEADS = 4
QD = 64
QUERY_BLOCK_ROWS = 512
QKVW = 5120


def paired_draw(key):
    queries = jnp.clip(jax.random.normal(jax.random.fold_in(key, 101), (QUERY_BLOCK_ROWS, QUERY_HEADS * HEAD_SIZE), jnp.float32), -6.0, 6.0)
    keys = jnp.clip(jax.random.normal(jax.random.fold_in(key, 202), (QUERY_BLOCK_ROWS, KEY_VALUE_HEADS * HEAD_SIZE), jnp.float32), -6.0, 6.0)
    head_place = jnp.arange(QUERY_HEADS, dtype=jnp.float32) / max(QUERY_HEADS - 1, 1)
    jitter = jax.random.uniform(jax.random.fold_in(key, 505), (QUERY_HEADS,), jnp.float32, 0.85, 1.15)
    head_scale = 0.6 * jnp.exp(head_place * math.log(6.0)) * jitter
    queries = queries * jnp.repeat(head_scale, HEAD_SIZE)[None, :]
    queries = jnp.clip(queries, -128.0, 128.0)
    return (queries, keys)


def draw_queries(key, part):
    return paired_draw(key)[0].astype(jnp.bfloat16)


def draw_keys(key, part):
    return paired_draw(key)[1].astype(jnp.bfloat16)


def retained_sequence_pick(key):
    base = jax.random.fold_in(key, 404)
    shard_count = QUERY_BLOCK_ROWS // QD
    levels = jax.random.randint(jax.random.fold_in(base, 1), (shard_count,), 0, 4)
    full_shard = jax.random.randint(jax.random.fold_in(base, 2), (), 0, shard_count)
    levels = jnp.where(jnp.arange(shard_count, dtype=jnp.int32) == full_shard, 5, levels)
    noise = jax.random.randint(jax.random.fold_in(base, 3), (QUERY_BLOCK_ROWS,), 0, 1024)
    position = jnp.arange(QUERY_BLOCK_ROWS, dtype=jnp.int32)
    ranking = (jnp.repeat(levels, QD) * 1024 + noise) * QUERY_BLOCK_ROWS + position
    unused, picked = lax.top_k(ranking, QUERY_BLOCK_ROWS // 2)
    marked = jnp.zeros((QUERY_BLOCK_ROWS,), jnp.int32).at[picked].set(1).reshape(shard_count, QD)
    counts = jnp.sum(marked, axis=1).astype(jnp.int32)
    partition_inner_position = jnp.arange(QD, dtype=jnp.int32)
    order_key = (1 - marked) * QD + partition_inner_position[None, :]
    ordered = jnp.argsort(order_key, axis=1, stable=True).astype(jnp.int32)
    retained_lists = jnp.where(partition_inner_position[None, :] < counts[:, None], ordered, -1).reshape(QUERY_BLOCK_ROWS)
    return (retained_lists, counts)


def draw_retained_lists(key, part):
    return retained_sequence_pick(key)[0]


def draw_counts(key, part):
    return retained_sequence_pick(key)[1]


def shard_levels(stream_key, dims, split, smallest, largest):
    level, own = 1.0, jax.random.fold_in(stream_key, 6)
    for axis_at, blocks in split:
        heights = jnp.exp(jax.random.uniform(jax.random.fold_in(own, axis_at), (blocks,), jnp.float32, smallest / len(split), largest / len(split)))
        level = level * jnp.repeat(heights, dims[axis_at] // blocks).reshape([-1 if axis == axis_at else 1 for axis in range(len(dims))])
    return level


def gaussian(rng, extent, width, limit, pieces=(), kind=jnp.bfloat16):
    entries = jax.random.normal(rng, extent, jnp.float32) * width
    if len(pieces) > 0:
        entries = shard_levels(rng, extent, pieces, -0.22, 0.18) * entries
    return jnp.clip(entries, min=-limit, max=limit).astype(kind)


def setup_inputs(seed: int = 0, part: int = 0) -> dict:
    arg_keys = jax.random.split(jax.random.key(seed), 10)
    part_keys = jax.random.split(jax.random.fold_in(arg_keys[9], part), 10)
    return {
        "queries": draw_queries(jax.random.fold_in(jax.random.fold_in(arg_keys[9], part), 71), part),
        "keys": draw_keys(jax.random.fold_in(jax.random.fold_in(arg_keys[9], part), 71), part),
        "values": gaussian(part_keys[2], (QUERY_BLOCK_ROWS, KEY_VALUE_HEADS * HEAD_SIZE), 1.0, 6.0, ((0, 8), (1, 2))),
        "hidden": gaussian(part_keys[3], (QUERY_BLOCK_ROWS, D), 1.0, 6.0, ((0, 8),)),
        "norm_gain": jnp.clip(1.0 + 0.18 * jax.random.normal(arg_keys[4], (D,), jnp.float32), 0.1, 1.9),
        "retained_lists": draw_retained_lists(jax.random.fold_in(jax.random.fold_in(arg_keys[9], part), 71), part),
        "counts": draw_counts(jax.random.fold_in(jax.random.fold_in(arg_keys[9], part), 71), part),
        "affine_matrix": gaussian(arg_keys[7], (D, QKVW), D ** -0.5, 0.0625, ((0, 8), (1, 2))),
        "affine_offset_vector": gaussian(arg_keys[8], (QKVW,), 0.5, 3.0, ((0, 2),), jnp.float32),
    }


def reference(queries, keys, values, hidden, norm_gain, retained_lists, counts, affine_matrix, affine_offset_vector):
    asker_line_tile = queries.shape[0]
    group_width = QUERY_HEADS // KEY_VALUE_HEADS
    positions = jnp.arange(asker_line_tile, dtype=jnp.int32)
    allowed = positions[None, :] <= positions[:, None]
    query_heads = queries.reshape(asker_line_tile, QUERY_HEADS, HEAD_SIZE).transpose(1, 0, 2)
    key_head_rows = keys.reshape(asker_line_tile, KEY_VALUE_HEADS, HEAD_SIZE).transpose(1, 0, 2)
    value_head_rows = values.reshape(asker_line_tile, KEY_VALUE_HEADS, HEAD_SIZE).transpose(1, 0, 2)

    def one_head(head):
        kv_index = head // group_width
        query_one = lax.dynamic_index_in_dim(query_heads, head, 0, keepdims=False)
        key_one = lax.dynamic_index_in_dim(key_head_rows, kv_index, 0, keepdims=False)
        value_one = lax.dynamic_index_in_dim(value_head_rows, kv_index, 0, keepdims=False)
        scores = jnp.dot(query_one, key_one.T, preferred_element_type=jnp.float32) * HEAD_SIZE ** (-0.5)
        row_max = lax.optimization_barrier(jnp.max(jnp.where(allowed, scores, -1e+30), axis=1))
        weights = jnp.where(allowed, jnp.exp(scores - row_max[:, None]), 0.0)
        row_sum = lax.optimization_barrier(jnp.sum(weights, axis=1))
        mixed = jnp.dot(weights.astype(jnp.bfloat16), value_one, preferred_element_type=jnp.float32) / row_sum[:, None]
        column = lax.optimization_barrier(jnp.sum(weights / row_sum[:, None], axis=0))
        return (mixed, column)
    mixed_all, columns = lax.map(one_head, jnp.arange(QUERY_HEADS, dtype=jnp.int32))
    context = mixed_all.transpose(1, 0, 2).reshape(asker_line_tile, QUERY_HEADS * HEAD_SIZE)
    col_scores = lax.optimization_barrier(jnp.sum(columns, axis=0)) / QUERY_HEADS
    hidden_f = hidden.astype(jnp.float32)
    rescaled_activations = (hidden_f * lax.rsqrt(lax.optimization_barrier(jnp.mean(hidden_f * hidden_f, axis=1, keepdims=True)) + 1e-06) * norm_gain).astype(jnp.bfloat16)
    shard_count = counts.shape[0]
    partition_inner_lines = asker_line_tile // shard_count
    retained_total = asker_line_tile // 2
    retained_element = jnp.arange(retained_total, dtype=jnp.int32)
    partition_finish_marks = jnp.cumsum(counts).astype(jnp.int32)
    holder_partition = lax.optimization_barrier(jnp.sum((partition_finish_marks[None, :] <= retained_element[:, None]).astype(jnp.int32), axis=1))
    starts = partition_finish_marks - counts
    opening_marks = lax.optimization_barrier(jnp.sum(jnp.where(jnp.arange(shard_count, dtype=jnp.int32)[None, :] == holder_partition[:, None], starts[None, :], 0), axis=1))
    retained_place_number = retained_element - opening_marks
    partition_inner_position = retained_lists[holder_partition * partition_inner_lines + retained_place_number]
    retained_elements = rescaled_activations[holder_partition * partition_inner_lines + partition_inner_position]
    tier_third_mapped_triples = jnp.dot(retained_elements, affine_matrix, preferred_element_type=jnp.float32) + affine_offset_vector
    return (context, col_scores, tier_third_mapped_triples)
```

```python
import functools
import math

import jax
import jax.numpy as jnp
from jax import lax
from jax.experimental import pallas as pl
from jax.experimental.pallas import tpu as pltpu
from jax.sharding import PartitionSpec as P

HEAD_SIZE = 128
QUERY_HEADS = 32
F32 = jnp.float32
BF16 = jnp.bfloat16


def remote(src, dst, send_sem, recv_sem, where):
    return pltpu.make_async_remote_copy(
        src_ref=src,
        dst_ref=dst,
        send_sem=send_sem,
        recv_sem=recv_sem,
        device_id=where,
        device_id_type=pl.DeviceIdType.MESH,
    )


def kernel(
    n, plan,
    q_hbm, k_hbm, v_hbm, h_hbm, gain_hbm, list_hbm, count_hbm, a_hbm, bias_hbm,
    ctx_ref, col_ref, out_ref,
    q_ref, h_ref, gain_ref, list_ref, count_ref, bias_ref, a_ref,
    kvbuf, s_ref, e_ref, raw_ref, norm_ref, note_send, note_recv, g_ref, comp_ref,
    s1_ref, r1_ref, own_ref, s2_ref, r2_ref, s3_ref, r3_ref,
    c_send, c_recv, ct_send, ct_recv,
    in_sem, a_sem, kz_ssem, kz_rsem, ky_ssem, ky_rsem, sv_ssem, sv_rsem, nt_ssem, nt_rsem,
    fw_ssem, fw_rsem, rs_ssem, rs_rsem, c_ssem, c_rsem, ct_ssem, ct_rsem,
):
    me = lax.axis_index("seq")
    ten = lax.axis_index("ten")
    sibling = {"ten": 1 - ten}
    rows = q_ref.shape[0]
    key_total = n * rows
    kv_heads = k_hbm.shape[1] // HEAD_SIZE
    group = q_ref.shape[1] // k_hbm.shape[1]
    width = h_ref.shape[1]
    half = width // n // 2
    out_rows = out_ref.shape[0]
    pairs = n // 2
    quads = pairs // 2
    quad_rows = quads * out_rows
    parity = lax.rem(me, 2)
    pair = lax.div(me, 2)
    partner = {"seq": me + 1 - 2 * parity}
    pair_parity = lax.rem(pair, 2)
    other_pair = pair + 1 - 2 * pair_parity
    other = {"seq": 2 * other_pair + parity}

    def block_columns(owner, side):
        return pl.ds(pl.multiple_of(owner * (2 * half) + side * half, 128), half)

    h_copy = pltpu.make_async_copy(h_hbm, h_ref, in_sem.at[0])
    h_copy.start()
    barrier = pltpu.get_barrier_semaphore()
    for d in range(1, n):
        pl.semaphore_signal(
            barrier, inc=1, device_id={"seq": lax.rem(me + d, n)},
            device_id_type=pl.DeviceIdType.MESH,
        )
    pl.semaphore_signal(
        barrier, inc=1, device_id=sibling, device_id_type=pl.DeviceIdType.MESH
    )
    kv_copies = [
        pltpu.make_async_copy(k_hbm, kvbuf.at[me, 0], in_sem.at[1]),
        pltpu.make_async_copy(v_hbm, kvbuf.at[me, 1], in_sem.at[2]),
    ]
    note_copies = [
        pltpu.make_async_copy(list_hbm, list_ref, in_sem.at[3]),
        pltpu.make_async_copy(count_hbm, count_ref, in_sem.at[4]),
    ]
    own_copies = [
        pltpu.make_async_copy(
            h_hbm.at[:, block_columns(me, side)], raw_ref.at[side, 0], in_sem.at[5 + side]
        )
        for side in range(2)
    ] + [
        pltpu.make_async_copy(
            gain_hbm.at[:, block_columns(me, side)], gain_ref.at[side], in_sem.at[7 + side]
        )
        for side in range(2)
    ]
    late_copies = [
        pltpu.make_async_copy(q_hbm, q_ref, in_sem.at[9]),
        pltpu.make_async_copy(bias_hbm, bias_ref, in_sem.at[10]),
    ]
    a_copy = pltpu.make_async_copy(a_hbm, a_ref, a_sem)
    for copy in kv_copies + note_copies + own_copies:
        copy.start()
    pl.semaphore_wait(barrier, n)

    def chain(age):
        block = kvbuf.at[2 * (pair - age) + parity]
        target = {"seq": me + 2}
        return remote(block, block, kz_ssem.at[age], kz_rsem.at[age + 1], target)

    def chain_in(age):
        block = kvbuf.at[2 * (pair - age) + parity]
        return remote(block, block, kz_ssem.at[age - 1], kz_rsem.at[age], partner)

    def across(age):
        block = kvbuf.at[2 * (pair - age) + parity]
        return remote(block, block, ky_ssem.at[age], ky_rsem.at[age], partner)

    def across_in(age):
        block = kvbuf.at[2 * (pair - age) + 1 - parity]
        return remote(block, block, ky_ssem.at[age], ky_rsem.at[age], partner)

    def relay(age):
        @pl.when(pair >= age)
        def _():
            chain_in(age).wait_recv()

            @pl.when(pair + 1 < pairs)
            def _():
                if age + 1 < pairs:
                    chain(age).start()

            across(age).start()

    def raw_copy(d, target):
        return remote(
            h_ref.at[:, block_columns(target, ten)], raw_ref.at[ten, d],
            sv_ssem.at[d], sv_rsem.at[d], {"seq": target},
        )

    def note_copy(d, target):
        return remote(
            note_send, note_recv.at[d], nt_ssem.at[d], nt_rsem.at[d], {"seq": target}
        )

    def forward(d, side):
        block = raw_ref.at[side, d]
        return remote(block, block, fw_ssem.at[d], fw_rsem.at[d], sibling)

    order = sorted(range(1, n), key=lambda d: abs(2 * d - n))
    first_sends = 2
    lag = 3
    for copy in kv_copies:
        copy.wait()

    @pl.when(pair + 1 < pairs)
    def _():
        chain(0).start()

    h_copy.wait()
    for d in order[:first_sends]:
        raw_copy(d, lax.rem(me + d, n)).start()

    @pl.when(parity == 0)
    def _():
        across(0).start()

    lane = lax.broadcasted_iota(jnp.int32, (rows, rows), 1)
    line = lax.broadcasted_iota(jnp.int32, (rows, rows), 0)
    for copy in note_copies:
        copy.wait()
    shard_at = lax.broadcasted_iota(jnp.int32, (1, n), 1)
    opening = jnp.sum(
        jnp.where(shard_at < me, count_ref[...], 0), axis=1, keepdims=True
    )
    kept = jnp.sum(jnp.where(lane == line, list_ref[...], 0), axis=1, keepdims=True)
    place = jnp.sum(
        jnp.where(kept == lane, opening + line + 1, 0), axis=0, keepdims=True
    ) - 1
    square = jnp.zeros((rows, 1), F32)
    step = math.gcd(width, 1024)
    for c in range(width // step):
        x = h_ref[:, c * step:(c + 1) * step].astype(F32)
        square = square + jnp.sum(x * x, axis=1, keepdims=True)
    rescale = lax.rsqrt(square / width + 1e-06)
    note_send[...] = jnp.zeros_like(note_send)
    note_send[0:1, :rows] = jnp.sum(
        jnp.where(lane == line, rescale, 0.0), axis=0, keepdims=True
    )
    note_send[1:2, :rows] = place.astype(F32)
    note_recv[0] = note_send[...]
    for d in order:
        note_copy(d, lax.rem(me + d, n)).start()
    relay(1)
    for d in order[first_sends:]:
        raw_copy(d, lax.rem(me + d, n)).start()
    a_copy.start()
    for copy in late_copies:
        copy.start()

    def clear(j, carry):
        kvbuf[j] = jnp.zeros_like(kvbuf[j])
        return carry

    lax.fori_loop(me + 1, n, clear, 0)
    for copy in own_copies:
        copy.wait()

    def normalise(d):
        scale = jnp.sum(
            jnp.where(lane == line, note_recv[d, 0:1, :rows], 0.0), axis=1, keepdims=True
        )
        for side in range(2):
            x = raw_ref[side, d].astype(F32) * scale * gain_ref[side]
            norm_ref[side, d * rows:(d + 1) * rows, :] = x.astype(BF16)

    def settle(d):
        forward(d, 1 - ten).wait_recv()
        normalise(d)

    normalise(0)
    for at, d in enumerate(order):
        raw_copy(d, me).wait_recv()
        forward(d, ten).start()
        if at % 2 == 0 and 0 < at < n - 2:
            relay(at // 2 + 1)
        note_copy(d, me).wait_recv()
        if at >= lag:
            settle(order[at - lag])

    places = jnp.concatenate(
        [note_recv[d, 1:2, :rows] for d in range(n)], axis=1
    ).astype(jnp.int32)
    row_at = lax.broadcasted_iota(jnp.int32, (out_rows, key_total), 0)
    for side in range(2):
        side_parity = 1 - parity if side == 0 else parity
        for d in range(pairs):
            origin = other_pair if d < quads else pair
            base = (2 * lax.rem(origin + 2 * (d % quads), pairs) + side_parity) * out_rows
            first = (side * pairs + d) * out_rows
            g_ref[first:first + out_rows, :] = (
                (row_at + base == places).astype(F32).astype(BF16)
            )
    for d in order[-lag:]:
        settle(d)
    for side in range(2):
        comp_ref[:, side * half:(side + 1) * half] = jnp.dot(
            g_ref[...], norm_ref[side], preferred_element_type=F32
        ).astype(BF16)
    a_copy.wait()

    half_rows = 2 * quad_rows

    def rs_copy(c, slot, src, dst, target):
        return remote(src, dst, rs_ssem.at[c, slot], rs_rsem.at[c, slot], target)

    def lines(ref, c, first, count):
        start, size = plan[c][1:]
        return ref.at[first:first + count, start:start + size]

    def step_one(c):
        target = other if plan[c][0] == "W" else partner
        return rs_copy(
            c, 0, lines(s1_ref, c, 0, half_rows), lines(r1_ref, c, 0, half_rows), target
        )

    def step_two(c):
        kind = plan[c][0]
        if kind == "Y":
            return [rs_copy(
                c, 1, lines(s2_ref, c, 0, quad_rows), lines(r2_ref, c, 0, quad_rows), other
            )]
        copies = []
        if kind == "D":
            for j in sorted(range(pairs), key=lambda j: j % quads, reverse=True):
                if j != quads:
                    base = other_pair if j < quads else pair
                    target = {"seq": 2 * lax.rem(base + 2 * (j % quads), pairs) + parity}
                    copies.append(rs_copy(
                        c, 1 + j, lines(s2_ref, c, j * out_rows, out_rows),
                        lines(r2_ref, c, j * out_rows, out_rows), target,
                    ))
        else:
            for d in range(1, quads):
                target = {"seq": 2 * lax.rem(pair + 2 * d, pairs) + parity}
                copies.append(rs_copy(
                    c, 1 + d, lines(s2_ref, c, 2 * d * out_rows, 2 * out_rows),
                    lines(r2_ref, c, 2 * d * out_rows, 2 * out_rows), target,
                ))
        return copies

    def step_three(c):
        kind = plan[c][0]
        if kind == "D":
            return []
        if kind == "W":
            return [rs_copy(
                c, 1 + pairs, lines(s3_ref, c, 0, out_rows), lines(r3_ref, c, 0, out_rows),
                partner,
            )]
        return [
            rs_copy(
                c, 1 + pairs + d, lines(s3_ref, c, d * out_rows, out_rows),
                lines(r3_ref, c, d * out_rows, out_rows),
                {"seq": 2 * lax.rem(pair + 2 * d, pairs) + parity},
            )
            for d in range(1, quads)
        ]

    def columns_of(c):
        return slice(plan[c][1], plan[c][1] + plan[c][2])

    def after_one(c):
        kind, cols = plan[c][0], columns_of(c)
        step_one(c).wait_recv()
        if kind == "Y":
            s2_ref[:quad_rows, cols] = (
                own_ref[:quad_rows, cols] + r1_ref[:quad_rows, cols].astype(F32)
            ).astype(BF16)
        elif kind == "D":
            for j in range(pairs):
                if j != quads:
                    part = slice(j * out_rows, (j + 1) * out_rows)
                    s2_ref[part, cols] = (
                        own_ref[part, cols] + r1_ref[part, cols].astype(F32)
                    ).astype(BF16)
        else:
            for d in range(1, quads):
                for q in range(2):
                    part = slice(q * quad_rows + d * out_rows, q * quad_rows + (d + 1) * out_rows)
                    place_at = (2 * d + q) * out_rows
                    s2_ref[place_at:place_at + out_rows, cols] = (
                        own_ref[part, cols] + r1_ref[part, cols].astype(F32)
                    ).astype(BF16)
        for copy in step_two(c):
            copy.start()

    def after_two(c):
        kind, cols = plan[c][0], columns_of(c)
        for copy in step_two(c):
            copy.wait_recv()
        if kind == "Y":
            for d in range(1, quads):
                part = slice(quad_rows + d * out_rows, quad_rows + (d + 1) * out_rows)
                s3_ref[d * out_rows:(d + 1) * out_rows, cols] = (
                    own_ref[part, cols]
                    + r1_ref[part, cols].astype(F32)
                    + r2_ref[d * out_rows:(d + 1) * out_rows, cols].astype(F32)
                ).astype(BF16)
        elif kind == "W":
            total = own_ref[:out_rows, cols] + r1_ref[:out_rows, cols].astype(F32)
            for d in range(1, quads):
                first = 2 * d * out_rows
                total = total + r2_ref[first:first + out_rows, cols].astype(F32)
            s3_ref[:out_rows, cols] = total.astype(BF16)
        for copy in step_three(c):
            copy.start()

    def finish(c):
        kind, cols = plan[c][0], columns_of(c)
        for copy in step_three(c):
            copy.wait_recv()
        mine = slice(quad_rows, quad_rows + out_rows)
        total = own_ref[mine, cols] + r1_ref[mine, cols].astype(F32)
        if kind == "Y":
            total = total + r2_ref[:out_rows, cols].astype(F32)
            for d in range(1, quads):
                total = total + r3_ref[d * out_rows:(d + 1) * out_rows, cols].astype(F32)
        elif kind == "D":
            for j in range(pairs):
                if j != quads:
                    total = total + r2_ref[j * out_rows:(j + 1) * out_rows, cols].astype(F32)
        else:
            for d in range(1, quads):
                first = (2 * d + 1) * out_rows
                total = total + r2_ref[first:first + out_rows, cols].astype(F32)
            total = total + r3_ref[:out_rows, cols].astype(F32)
        out_ref[:, cols] = total + bias_ref[cols].reshape(1, plan[c][2])

    for c in range(len(plan)):
        cols = columns_of(c)
        part = jnp.dot(comp_ref[...], a_ref[:, cols], preferred_element_type=F32)
        quarters = [part[i * quad_rows:(i + 1) * quad_rows] for i in range(4)]
        away, stay = ((0, 2), (1, 3)) if plan[c][0] == "W" else ((0, 1), (2, 3))
        for i in range(2):
            s1_ref[i * quad_rows:(i + 1) * quad_rows, cols] = quarters[away[i]].astype(BF16)
        step_one(c).start()
        for i in range(2):
            own_ref[i * quad_rows:(i + 1) * quad_rows, cols] = quarters[stay[i]]

    def await_keys():
        @pl.when(parity == 1)
        def _():
            across_in(0).wait_recv()

        for age in range(1, pairs):

            @pl.when(pair >= age)
            def _():
                across_in(age).wait_recv()

        for copy in late_copies:
            copy.wait()

    def attend(h, columns_total):
        key_pos = lax.broadcasted_iota(jnp.int32, (rows, key_total), 1)
        query_pos = me * rows + lax.broadcasted_iota(jnp.int32, (rows, key_total), 0)
        allowed = key_pos <= query_pos
        heads = slice(h * HEAD_SIZE, (h + 1) * HEAD_SIZE)
        query = jnp.concatenate(
            [
                q_ref[:, (h * group + a) * HEAD_SIZE:(h * group + a + 1) * HEAD_SIZE]
                for a in range(group)
            ],
            axis=0,
        )
        key = kvbuf[:, 0, :, heads].reshape(key_total, HEAD_SIZE)
        value = kvbuf[:, 1, :, heads].reshape(key_total, HEAD_SIZE)
        s_ref[...] = lax.dot_general(
            query, key, (((1,), (1,)), ((), ())), preferred_element_type=F32
        )
        inverses = []
        for a in range(group):
            part = slice(a * rows, (a + 1) * rows)
            scores = jnp.where(allowed, s_ref[part, :] * HEAD_SIZE ** (-0.5), -1e30)
            largest = jnp.max(scores, axis=1, keepdims=True)
            weights = jnp.where(allowed, jnp.exp(scores - largest), 0.0)
            e_ref[part, :] = weights.astype(BF16)
            inverse = 1.0 / jnp.sum(weights, axis=1, keepdims=True)
            inverses.append(inverse)
            columns_total = columns_total + jnp.sum(
                (weights * inverse).reshape(rows // 8, 8, key_total), axis=0
            )
        mixed = jnp.dot(e_ref[...], value, preferred_element_type=F32)
        for a in range(group):
            place_at = (h * group + a) * HEAD_SIZE
            ctx_ref[:, place_at:place_at + HEAD_SIZE] = (
                mixed[a * rows:(a + 1) * rows] * inverses[a]
            )
        return columns_total

    lanes = c_send.shape[2]
    per = lanes // rows

    def col_copy(d, owner, target):
        return remote(
            c_send.at[lax.div(owner, per)], c_recv.at[d], c_ssem.at[d], c_rsem.at[d],
            {"seq": target},
        )

    def send_columns(columns_total):
        for b in range(n // per):
            c_send[b] = columns_total[:, b * lanes:(b + 1) * lanes]
        for d in range(1, n):

            @pl.when(me - d >= 0)
            def _():
                col_copy(d, me - d, me - d).start()

    ct = remote(ct_send, ct_recv, ct_ssem, ct_rsem, sibling)

    def sum_columns():
        mine = c_send[lax.div(me, per)]
        for d in range(1, n):
            c_recv_valid = me + d < n

            @pl.when(c_recv_valid)
            def _():
                col_copy(d, me, me).wait_recv()

            @pl.when(jnp.logical_not(c_recv_valid))
            def _():
                c_recv[d] = jnp.zeros_like(c_recv[d])

            mine = mine + c_recv[d]
        ct_send[...] = mine
        ct.start()

    state = {"columns": jnp.zeros((8, key_total), F32)}

    def attention(h):
        if h == 0:
            await_keys()
        state["columns"] = attend(h, state["columns"])
        if h == kv_heads - 1:
            send_columns(state["columns"])

    after_one(0)
    after_one(1)
    after_two(0)
    after_two(1)
    for h in range(kv_heads):
        if h == kv_heads - 1:
            after_one(2)
        attention(h)
    after_one(3)
    after_two(2)
    after_one(4)
    sum_columns()
    for c in range(len(plan)):
        if plan[c][0] == "D":
            after_two(c)
        finish(c)

    ct.wait()
    both = jnp.sum(ct_send[...] + ct_recv[...], axis=0, keepdims=True) / QUERY_HEADS
    turn = lax.rem(me, per)
    picked = both[:, :rows]
    for b in range(1, per):
        picked = jnp.where(turn == b, both[:, b * rows:(b + 1) * rows], picked)
    col_ref[...] = picked

    for d in range(1, n):

        @pl.when(me - d >= 0)
        def _():
            col_copy(d, me - d, me - d).wait_send()

        raw_copy(d, lax.rem(me + d, n)).wait_send()
        note_copy(d, lax.rem(me + d, n)).wait_send()
        forward(d, ten).wait_send()

    @pl.when(parity == 0)
    def _():
        across(0).wait_send()

    @pl.when(pair + 1 < pairs)
    def _():
        chain(0).wait_send()

    for age in range(1, pairs):

        @pl.when(pair >= age)
        def _():
            across(age).wait_send()

        if age + 1 < pairs:

            @pl.when((pair >= age) & (pair + 1 < pairs))
            def _():
                chain(age).wait_send()

    for c in range(len(plan)):
        for copy in [step_one(c)] + step_two(c) + step_three(c):
            copy.wait_send()


def hand_over(context, scores, projected, context_out, scores_out, projected_out):
    context_out[...] = context[...]
    scores_out[...] = scores[...]
    projected_out[...] = projected[...]


def shards(
    n, queries, keys, values, hidden, norm_gain, retained_lists, counts, affine_matrix,
    affine_offset_vector,
):
    rows, query_width = queries.shape
    width = hidden.shape[1]
    depth, columns = affine_matrix.shape
    kv_width = keys.shape[1]
    group = query_width // kv_width
    half = width // n // 2
    out_rows = rows // 2
    kept_total = n * out_rows
    pairs = n // 2
    quads = n // 4
    lanes = max(128, rows)
    key_total = n * rows
    plan, start = [], 0
    unit = columns // 20
    for kind, share in (("W", 4), ("Y", 5), ("Y", 5), ("D", 4), ("D", 2)):
        plan.append((kind, start, share * unit))
        start += share * unit
    chunks = len(plan)
    vmem = pl.BlockSpec(memory_space=pltpu.VMEM)
    hbm = pl.BlockSpec(memory_space=pltpu.HBM)
    dma = pltpu.SemaphoreType.DMA
    context, col_scores, projected = pl.pallas_call(
        functools.partial(kernel, n, tuple(plan)),
        out_shape=(
            pltpu.VMEM((rows, query_width), F32),
            pltpu.VMEM((1, rows), F32),
            pltpu.VMEM((out_rows, columns), F32),
        ),
        in_specs=[hbm] * 9,
        out_specs=(vmem, vmem, vmem),
        scratch_shapes=[
            pltpu.VMEM((rows, query_width), BF16),
            pltpu.VMEM((rows, width), BF16),
            pltpu.VMEM((2, 1, half), F32),
            pltpu.VMEM((1, rows), jnp.int32),
            pltpu.VMEM((1, n), jnp.int32),
            pltpu.VMEM((columns,), F32),
            pltpu.VMEM((depth, columns), BF16),
            pltpu.VMEM((n, 2, rows, kv_width), BF16),
            pltpu.VMEM((group * rows, key_total), F32),
            pltpu.VMEM((group * rows, key_total), BF16),
            pltpu.VMEM((2, n, rows, half), BF16),
            pltpu.VMEM((2, key_total, half), BF16),
            pltpu.VMEM((8, lanes), F32),
            pltpu.VMEM((n, 8, lanes), F32),
            pltpu.VMEM((kept_total, key_total), BF16),
            pltpu.VMEM((kept_total, 2 * half), BF16),
            pltpu.VMEM((kept_total // 2, columns), BF16),
            pltpu.VMEM((kept_total // 2, columns), BF16),
            pltpu.VMEM((kept_total // 2, columns), F32),
            pltpu.VMEM((kept_total // 2, columns), BF16),
            pltpu.VMEM((kept_total // 2, columns), BF16),
            pltpu.VMEM((kept_total // 4, columns), BF16),
            pltpu.VMEM((kept_total // 4, columns), BF16),
            pltpu.VMEM((key_total // lanes, 8, lanes), F32),
            pltpu.VMEM((n, 8, lanes), F32),
            pltpu.VMEM((8, lanes), F32),
            pltpu.VMEM((8, lanes), F32),
            dma((11,)),
            dma,
            dma((pairs,)), dma((pairs,)),
            dma((pairs,)), dma((pairs,)),
            dma((n,)), dma((n,)),
            dma((n,)), dma((n,)),
            dma((n,)), dma((n,)),
            dma((chunks, 1 + pairs + quads)), dma((chunks, 1 + pairs + quads)),
            dma((n,)), dma((n,)),
            dma, dma,
        ],
        compiler_params=pltpu.CompilerParams(
            collective_id=0, has_side_effects=True, vmem_limit_bytes=56 * 2 ** 20
        ),
    )(
        queries, keys, values, hidden, norm_gain.reshape(1, width),
        retained_lists.reshape(1, rows), counts.reshape(1, n), affine_matrix,
        affine_offset_vector,
    )
    context, col_scores, projected = pl.pallas_call(
        hand_over,
        out_shape=(
            jax.ShapeDtypeStruct(context.shape, F32),
            jax.ShapeDtypeStruct(col_scores.shape, F32),
            jax.ShapeDtypeStruct(projected.shape, F32),
        ),
        in_specs=[vmem, vmem, vmem],
        out_specs=(vmem, vmem, vmem),
        compiler_params=pltpu.CompilerParams(vmem_limit_bytes=8 * 2 ** 20),
    )(context, col_scores, projected)
    return (context, col_scores.reshape(rows), projected)


def solution(mesh):
    in_specs = (
        P(("grp", "seq"), "ten"),
        P(("grp", "seq"), "ten"),
        P(("grp", "seq"), "ten"),
        P(("grp", "seq"), None),
        P(),
        P(("grp", "seq")),
        P("grp"),
        P("seq", "ten"),
        P("ten"),
    )
    out_specs = (P(("grp", "seq"), "ten"), P(("grp", "seq")), P(("grp", "seq"), "ten"))
    return jax.shard_map(
        functools.partial(shards, mesh.shape["seq"]),
        mesh=mesh, in_specs=in_specs, out_specs=out_specs, check_vma=False,
    )
```

```python
import functools
import math

import jax
import jax.numpy as jnp
from jax import lax
from jax.experimental import pallas as pl
from jax.experimental.pallas import tpu as pltpu
from jax.sharding import PartitionSpec as P

HEAD_SIZE = 128
QUERY_HEADS = 32
F32 = jnp.float32
BF16 = jnp.bfloat16


def remote(src, dst, send_sem, recv_sem, where):
    return pltpu.make_async_remote_copy(
        src_ref=src,
        dst_ref=dst,
        send_sem=send_sem,
        recv_sem=recv_sem,
        device_id=where,
        device_id_type=pl.DeviceIdType.MESH,
    )


def kernel(
    n, plan,
    q_hbm, k_hbm, v_hbm, h_hbm, gain_hbm, list_hbm, count_hbm, a_hbm, bias_hbm,
    ctx_ref, col_ref, out_ref,
    q_ref, h_ref, gain_ref, list_ref, count_ref, bias_ref, a_ref,
    kvbuf, s_ref, e_ref, raw_ref, norm_ref, note_send, note_recv, g_ref, comp_ref,
    s1_ref, r1_ref, own_ref, s2_ref, r2_ref, s3_ref, r3_ref,
    c_send, c_recv, ct_send, ct_recv,
    in_sem, a_sem, kz_ssem, kz_rsem, ky_ssem, ky_rsem, sv_ssem, sv_rsem, nt_ssem, nt_rsem,
    fw_ssem, fw_rsem, rs_ssem, rs_rsem, c_ssem, c_rsem, ct_ssem, ct_rsem,
):
    me = lax.axis_index("seq")
    ten = lax.axis_index("ten")
    sibling = {"ten": 1 - ten}
    rows = q_ref.shape[0]
    key_total = n * rows
    kv_heads = k_hbm.shape[1] // HEAD_SIZE
    group = q_ref.shape[1] // k_hbm.shape[1]
    width = h_ref.shape[1]
    half = width // n // 2
    out_rows = out_ref.shape[0]
    pairs = n // 2
    quads = pairs // 2
    quad_rows = quads * out_rows
    parity = lax.rem(me, 2)
    pair = lax.div(me, 2)
    partner = {"seq": me + 1 - 2 * parity}
    pair_parity = lax.rem(pair, 2)
    other_pair = pair + 1 - 2 * pair_parity
    other = {"seq": 2 * other_pair + parity}

    def block_columns(owner, side):
        return pl.ds(pl.multiple_of(owner * (2 * half) + side * half, 128), half)

    h_copy = pltpu.make_async_copy(h_hbm, h_ref, in_sem.at[0])
    h_copy.start()
    barrier = pltpu.get_barrier_semaphore()
    for d in range(1, n):
        pl.semaphore_signal(
            barrier, inc=1, device_id={"seq": lax.rem(me + d, n)},
            device_id_type=pl.DeviceIdType.MESH,
        )
    pl.semaphore_signal(
        barrier, inc=1, device_id=sibling, device_id_type=pl.DeviceIdType.MESH
    )
    kv_copies = [
        pltpu.make_async_copy(k_hbm, kvbuf.at[me, 0], in_sem.at[1]),
        pltpu.make_async_copy(v_hbm, kvbuf.at[me, 1], in_sem.at[2]),
    ]
    note_copies = [
        pltpu.make_async_copy(list_hbm, list_ref, in_sem.at[3]),
        pltpu.make_async_copy(count_hbm, count_ref, in_sem.at[4]),
    ]
    own_copies = [
        pltpu.make_async_copy(
            h_hbm.at[:, block_columns(me, side)], raw_ref.at[side, 0], in_sem.at[5 + side]
        )
        for side in range(2)
    ] + [
        pltpu.make_async_copy(
            gain_hbm.at[:, block_columns(me, side)], gain_ref.at[side], in_sem.at[7 + side]
        )
        for side in range(2)
    ]
    late_copies = [
        pltpu.make_async_copy(q_hbm, q_ref, in_sem.at[9]),
        pltpu.make_async_copy(bias_hbm, bias_ref, in_sem.at[10]),
    ]
    a_copy = pltpu.make_async_copy(a_hbm, a_ref, a_sem)
    for copy in kv_copies + note_copies + own_copies:
        copy.start()
    pl.semaphore_wait(barrier, n)

    def chain(age):
        block = kvbuf.at[2 * (pair - age) + parity]
        target = {"seq": me + 2}
        return remote(block, block, kz_ssem.at[age], kz_rsem.at[age + 1], target)

    def chain_in(age):
        block = kvbuf.at[2 * (pair - age) + parity]
        return remote(block, block, kz_ssem.at[age - 1], kz_rsem.at[age], partner)

    def across(age):
        block = kvbuf.at[2 * (pair - age) + parity]
        return remote(block, block, ky_ssem.at[age], ky_rsem.at[age], partner)

    def across_in(age):
        block = kvbuf.at[2 * (pair - age) + 1 - parity]
        return remote(block, block, ky_ssem.at[age], ky_rsem.at[age], partner)

    def relay(age):
        @pl.when(pair >= age)
        def _():
            chain_in(age).wait_recv()

            @pl.when(pair + 1 < pairs)
            def _():
                if age + 1 < pairs:
                    chain(age).start()

            across(age).start()

    def raw_copy(d, target):
        return remote(
            h_ref.at[:, block_columns(target, ten)], raw_ref.at[ten, d],
            sv_ssem.at[d], sv_rsem.at[d], {"seq": target},
        )

    def note_copy(d, target):
        return remote(
            note_send, note_recv.at[d], nt_ssem.at[d], nt_rsem.at[d], {"seq": target}
        )

    def forward(d, side):
        block = raw_ref.at[side, d]
        return remote(block, block, fw_ssem.at[d], fw_rsem.at[d], sibling)

    order = sorted(range(1, n), key=lambda d: abs(2 * d - n))
    first_sends = 2
    lag = 3
    for copy in kv_copies:
        copy.wait()

    @pl.when(pair + 1 < pairs)
    def _():
        chain(0).start()

    h_copy.wait()
    for d in order[:first_sends]:
        raw_copy(d, lax.rem(me + d, n)).start()

    @pl.when(parity == 0)
    def _():
        across(0).start()

    lane = lax.broadcasted_iota(jnp.int32, (rows, rows), 1)
    line = lax.broadcasted_iota(jnp.int32, (rows, rows), 0)
    for copy in note_copies:
        copy.wait()
    shard_at = lax.broadcasted_iota(jnp.int32, (1, n), 1)
    opening = jnp.sum(
        jnp.where(shard_at < me, count_ref[...], 0), axis=1, keepdims=True
    )
    kept = jnp.sum(jnp.where(lane == line, list_ref[...], 0), axis=1, keepdims=True)
    place = jnp.sum(
        jnp.where(kept == lane, opening + line + 1, 0), axis=0, keepdims=True
    ) - 1
    square = jnp.zeros((rows, 1), F32)
    step = math.gcd(width, 1024)
    for c in range(width // step):
        x = h_ref[:, c * step:(c + 1) * step].astype(F32)
        square = square + jnp.sum(x * x, axis=1, keepdims=True)
    rescale = lax.rsqrt(square / width + 1e-06)
    note_send[...] = jnp.zeros_like(note_send)
    note_send[0:1, :rows] = jnp.sum(
        jnp.where(lane == line, rescale, 0.0), axis=0, keepdims=True
    )
    note_send[1:2, :rows] = place.astype(F32)
    note_recv[0] = note_send[...]
    for d in order:
        note_copy(d, lax.rem(me + d, n)).start()
    relay(1)
    for d in order[first_sends:]:
        raw_copy(d, lax.rem(me + d, n)).start()
    a_copy.start()
    for copy in late_copies:
        copy.start()

    def clear(j, carry):
        kvbuf[j] = jnp.zeros_like(kvbuf[j])
        return carry

    lax.fori_loop(me + 1, n, clear, 0)
    for copy in own_copies:
        copy.wait()

    def normalise(d):
        scale = jnp.sum(
            jnp.where(lane == line, note_recv[d, 0:1, :rows], 0.0), axis=1, keepdims=True
        )
        for side in range(2):
            x = raw_ref[side, d].astype(F32) * scale * gain_ref[side]
            norm_ref[side, d * rows:(d + 1) * rows, :] = x.astype(BF16)

    def settle(d):
        forward(d, 1 - ten).wait_recv()
        normalise(d)

    normalise(0)
    for at, d in enumerate(order):
        raw_copy(d, me).wait_recv()
        forward(d, ten).start()
        if at % 2 == 0 and 0 < at < n - 2:
            relay(at // 2 + 1)
        note_copy(d, me).wait_recv()
        if at >= lag:
            settle(order[at - lag])

    places = jnp.concatenate(
        [note_recv[d, 1:2, :rows] for d in range(n)], axis=1
    ).astype(jnp.int32)
    row_at = lax.broadcasted_iota(jnp.int32, (out_rows, key_total), 0)
    for side in range(2):
        side_parity = 1 - parity if side == 0 else parity
        for d in range(pairs):
            origin = other_pair if d < quads else pair
            base = (2 * lax.rem(origin + 2 * (d % quads), pairs) + side_parity) * out_rows
            first = (side * pairs + d) * out_rows
            g_ref[first:first + out_rows, :] = (
                (row_at + base == places).astype(F32).astype(BF16)
            )
    for d in order[-lag:]:
        settle(d)
    for side in range(2):
        comp_ref[:, side * half:(side + 1) * half] = jnp.dot(
            g_ref[...], norm_ref[side], preferred_element_type=F32
        ).astype(BF16)
    a_copy.wait()

    half_rows = 2 * quad_rows

    def rs_copy(c, slot, src, dst, target):
        return remote(src, dst, rs_ssem.at[c, slot], rs_rsem.at[c, slot], target)

    def lines(ref, c, first, count):
        start, size = plan[c][1:]
        return ref.at[first:first + count, start:start + size]

    def step_one(c):
        target = other if plan[c][0] == "W" else partner
        return rs_copy(
            c, 0, lines(s1_ref, c, 0, half_rows), lines(r1_ref, c, 0, half_rows), target
        )

    def step_two(c):
        kind = plan[c][0]
        if kind == "Y":
            return [rs_copy(
                c, 1, lines(s2_ref, c, 0, quad_rows), lines(r2_ref, c, 0, quad_rows), other
            )]
        copies = []
        if kind == "D":
            for j in sorted(range(pairs), key=lambda j: j % quads, reverse=True):
                if j != quads:
                    base = other_pair if j < quads else pair
                    target = {"seq": 2 * lax.rem(base + 2 * (j % quads), pairs) + parity}
                    copies.append(rs_copy(
                        c, 1 + j, lines(s2_ref, c, j * out_rows, out_rows),
                        lines(r2_ref, c, j * out_rows, out_rows), target,
                    ))
        else:
            for d in range(1, quads):
                target = {"seq": 2 * lax.rem(pair + 2 * d, pairs) + parity}
                copies.append(rs_copy(
                    c, 1 + d, lines(s2_ref, c, 2 * d * out_rows, 2 * out_rows),
                    lines(r2_ref, c, 2 * d * out_rows, 2 * out_rows), target,
                ))
        return copies

    def step_three(c):
        kind = plan[c][0]
        if kind == "D":
            return []
        if kind == "W":
            return [rs_copy(
                c, 1 + pairs, lines(s3_ref, c, 0, out_rows), lines(r3_ref, c, 0, out_rows),
                partner,
            )]
        return [
            rs_copy(
                c, 1 + pairs + d, lines(s3_ref, c, d * out_rows, out_rows),
                lines(r3_ref, c, d * out_rows, out_rows),
                {"seq": 2 * lax.rem(pair + 2 * d, pairs) + parity},
            )
            for d in range(1, quads)
        ]

    def columns_of(c):
        return slice(plan[c][1], plan[c][1] + plan[c][2])

    def after_one(c):
        kind, cols = plan[c][0], columns_of(c)
        step_one(c).wait_recv()
        if kind == "Y":
            s2_ref[:quad_rows, cols] = (
                own_ref[:quad_rows, cols] + r1_ref[:quad_rows, cols].astype(F32)
            ).astype(BF16)
        elif kind == "D":
            for j in range(pairs):
                if j != quads:
                    part = slice(j * out_rows, (j + 1) * out_rows)
                    s2_ref[part, cols] = (
                        own_ref[part, cols] + r1_ref[part, cols].astype(F32)
                    ).astype(BF16)
        else:
            for d in range(1, quads):
                for q in range(2):
                    part = slice(q * quad_rows + d * out_rows, q * quad_rows + (d + 1) * out_rows)
                    place_at = (2 * d + q) * out_rows
                    s2_ref[place_at:place_at + out_rows, cols] = (
                        own_ref[part, cols] + r1_ref[part, cols].astype(F32)
                    ).astype(BF16)
        for copy in step_two(c):
            copy.start()

    def after_two(c):
        kind, cols = plan[c][0], columns_of(c)
        for copy in step_two(c):
            copy.wait_recv()
        if kind == "Y":
            for d in range(1, quads):
                part = slice(quad_rows + d * out_rows, quad_rows + (d + 1) * out_rows)
                s3_ref[d * out_rows:(d + 1) * out_rows, cols] = (
                    own_ref[part, cols]
                    + r1_ref[part, cols].astype(F32)
                    + r2_ref[d * out_rows:(d + 1) * out_rows, cols].astype(F32)
                ).astype(BF16)
        elif kind == "W":
            total = own_ref[:out_rows, cols] + r1_ref[:out_rows, cols].astype(F32)
            for d in range(1, quads):
                first = 2 * d * out_rows
                total = total + r2_ref[first:first + out_rows, cols].astype(F32)
            s3_ref[:out_rows, cols] = total.astype(BF16)
        for copy in step_three(c):
            copy.start()

    def finish(c):
        kind, cols = plan[c][0], columns_of(c)
        for copy in step_three(c):
            copy.wait_recv()
        mine = slice(quad_rows, quad_rows + out_rows)
        total = own_ref[mine, cols] + r1_ref[mine, cols].astype(F32)
        if kind == "Y":
            total = total + r2_ref[:out_rows, cols].astype(F32)
            for d in range(1, quads):
                total = total + r3_ref[d * out_rows:(d + 1) * out_rows, cols].astype(F32)
        elif kind == "D":
            for j in range(pairs):
                if j != quads:
                    total = total + r2_ref[j * out_rows:(j + 1) * out_rows, cols].astype(F32)
        else:
            for d in range(1, quads):
                first = (2 * d + 1) * out_rows
                total = total + r2_ref[first:first + out_rows, cols].astype(F32)
            total = total + r3_ref[:out_rows, cols].astype(F32)
        out_ref[:, cols] = total + bias_ref[cols].reshape(1, plan[c][2])

    for c in range(len(plan)):
        cols = columns_of(c)
        part = jnp.dot(comp_ref[...], a_ref[:, cols], preferred_element_type=F32)
        quarters = [part[i * quad_rows:(i + 1) * quad_rows] for i in range(4)]
        away, stay = ((0, 2), (1, 3)) if plan[c][0] == "W" else ((0, 1), (2, 3))
        for i in range(2):
            s1_ref[i * quad_rows:(i + 1) * quad_rows, cols] = quarters[away[i]].astype(BF16)
        step_one(c).start()
        for i in range(2):
            own_ref[i * quad_rows:(i + 1) * quad_rows, cols] = quarters[stay[i]]

    def await_keys():
        @pl.when(parity == 1)
        def _():
            across_in(0).wait_recv()

        for age in range(1, pairs):

            @pl.when(pair >= age)
            def _():
                across_in(age).wait_recv()

        for copy in late_copies:
            copy.wait()

    def attend(h, columns_total):
        key_pos = lax.broadcasted_iota(jnp.int32, (rows, key_total), 1)
        query_pos = me * rows + lax.broadcasted_iota(jnp.int32, (rows, key_total), 0)
        allowed = key_pos <= query_pos
        heads = slice(h * HEAD_SIZE, (h + 1) * HEAD_SIZE)
        query = jnp.concatenate(
            [
                q_ref[:, (h * group + a) * HEAD_SIZE:(h * group + a + 1) * HEAD_SIZE]
                for a in range(group)
            ],
            axis=0,
        )
        key = kvbuf[:, 0, :, heads].reshape(key_total, HEAD_SIZE)
        value = kvbuf[:, 1, :, heads].reshape(key_total, HEAD_SIZE)
        s_ref[...] = lax.dot_general(
            query, key, (((1,), (1,)), ((), ())), preferred_element_type=F32
        )
        inverses = []
        for a in range(group):
            part = slice(a * rows, (a + 1) * rows)
            scores = jnp.where(allowed, s_ref[part, :] * HEAD_SIZE ** (-0.5), -1e30)
            largest = jnp.max(scores, axis=1, keepdims=True)
            weights = jnp.where(allowed, jnp.exp(scores - largest), 0.0)
            e_ref[part, :] = weights.astype(BF16)
            inverse = 1.0 / jnp.sum(weights, axis=1, keepdims=True)
            inverses.append(inverse)
            columns_total = columns_total + jnp.sum(
                (weights * inverse).reshape(rows // 8, 8, key_total), axis=0
            )
        mixed = jnp.dot(e_ref[...], value, preferred_element_type=F32)
        for a in range(group):
            place_at = (h * group + a) * HEAD_SIZE
            ctx_ref[:, place_at:place_at + HEAD_SIZE] = (
                mixed[a * rows:(a + 1) * rows] * inverses[a]
            )
        return columns_total

    lanes = c_send.shape[2]
    per = lanes // rows

    def col_copy(d, owner, target):
        return remote(
            c_send.at[lax.div(owner, per)], c_recv.at[d], c_ssem.at[d], c_rsem.at[d],
            {"seq": target},
        )

    def send_columns(columns_total):
        for b in range(n // per):
            c_send[b] = columns_total[:, b * lanes:(b + 1) * lanes]
        for d in range(1, n):

            @pl.when(me - d >= 0)
            def _():
                col_copy(d, me - d, me - d).start()

    ct = remote(ct_send, ct_recv, ct_ssem, ct_rsem, sibling)

    def sum_columns():
        mine = c_send[lax.div(me, per)]
        for d in range(1, n):
            c_recv_valid = me + d < n

            @pl.when(c_recv_valid)
            def _():
                col_copy(d, me, me).wait_recv()

            @pl.when(jnp.logical_not(c_recv_valid))
            def _():
                c_recv[d] = jnp.zeros_like(c_recv[d])

            mine = mine + c_recv[d]
        ct_send[...] = mine
        ct.start()

    state = {"columns": jnp.zeros((8, key_total), F32)}

    def attention(h):
        if h == 0:
            await_keys()
        state["columns"] = attend(h, state["columns"])
        if h == kv_heads - 1:
            send_columns(state["columns"])

    after_one(1)
    after_one(0)
    attention(0)
    after_two(1)
    after_one(2)
    for h in range(1, kv_heads):
        attention(h)
    after_two(0)
    after_one(3)
    finish(1)
    after_one(4)
    after_two(2)
    sum_columns()
    after_one(5)
    after_two(3)
    finish(0)
    after_two(4)
    finish(4)
    finish(2)
    after_two(5)
    finish(5)
    finish(3)

    ct.wait()
    both = jnp.sum(ct_send[...] + ct_recv[...], axis=0, keepdims=True) / QUERY_HEADS
    turn = lax.rem(me, per)
    picked = both[:, :rows]
    for b in range(1, per):
        picked = jnp.where(turn == b, both[:, b * rows:(b + 1) * rows], picked)
    col_ref[...] = picked

    for d in range(1, n):

        @pl.when(me - d >= 0)
        def _():
            col_copy(d, me - d, me - d).wait_send()

        raw_copy(d, lax.rem(me + d, n)).wait_send()
        note_copy(d, lax.rem(me + d, n)).wait_send()
        forward(d, ten).wait_send()

    @pl.when(parity == 0)
    def _():
        across(0).wait_send()

    @pl.when(pair + 1 < pairs)
    def _():
        chain(0).wait_send()

    for age in range(1, pairs):

        @pl.when(pair >= age)
        def _():
            across(age).wait_send()

        if age + 1 < pairs:

            @pl.when((pair >= age) & (pair + 1 < pairs))
            def _():
                chain(age).wait_send()

    for c in range(len(plan)):
        for copy in [step_one(c)] + step_two(c) + step_three(c):
            copy.wait_send()


def hand_over(context, scores, projected, context_out, scores_out, projected_out):
    context_out[...] = context[...]
    scores_out[...] = scores[...]
    projected_out[...] = projected[...]


def shards(
    n, queries, keys, values, hidden, norm_gain, retained_lists, counts, affine_matrix,
    affine_offset_vector,
):
    rows, query_width = queries.shape
    width = hidden.shape[1]
    depth, columns = affine_matrix.shape
    kv_width = keys.shape[1]
    group = query_width // kv_width
    half = width // n // 2
    out_rows = rows // 2
    kept_total = n * out_rows
    pairs = n // 2
    quads = n // 4
    lanes = max(128, rows)
    key_total = n * rows
    plan, start = [], 0
    unit = columns // 20
    for kind, share in (("W", 4), ("Y", 3), ("Y", 4), ("Y", 4), ("D", 3), ("D", 2)):
        plan.append((kind, start, share * unit))
        start += share * unit
    chunks = len(plan)
    vmem = pl.BlockSpec(memory_space=pltpu.VMEM)
    hbm = pl.BlockSpec(memory_space=pltpu.HBM)
    dma = pltpu.SemaphoreType.DMA
    context, col_scores, projected = pl.pallas_call(
        functools.partial(kernel, n, tuple(plan)),
        out_shape=(
            pltpu.VMEM((rows, query_width), F32),
            pltpu.VMEM((1, rows), F32),
            pltpu.VMEM((out_rows, columns), F32),
        ),
        in_specs=[hbm] * 9,
        out_specs=(vmem, vmem, vmem),
        scratch_shapes=[
            pltpu.VMEM((rows, query_width), BF16),
            pltpu.VMEM((rows, width), BF16),
            pltpu.VMEM((2, 1, half), F32),
            pltpu.VMEM((1, rows), jnp.int32),
            pltpu.VMEM((1, n), jnp.int32),
            pltpu.VMEM((columns,), F32),
            pltpu.VMEM((depth, columns), BF16),
            pltpu.VMEM((n, 2, rows, kv_width), BF16),
            pltpu.VMEM((group * rows, key_total), F32),
            pltpu.VMEM((group * rows, key_total), BF16),
            pltpu.VMEM((2, n, rows, half), BF16),
            pltpu.VMEM((2, key_total, half), BF16),
            pltpu.VMEM((8, lanes), F32),
            pltpu.VMEM((n, 8, lanes), F32),
            pltpu.VMEM((kept_total, key_total), BF16),
            pltpu.VMEM((kept_total, 2 * half), BF16),
            pltpu.VMEM((kept_total // 2, columns), BF16),
            pltpu.VMEM((kept_total // 2, columns), BF16),
            pltpu.VMEM((kept_total // 2, columns), F32),
            pltpu.VMEM((kept_total // 2, columns), BF16),
            pltpu.VMEM((kept_total // 2, columns), BF16),
            pltpu.VMEM((kept_total // 4, columns), BF16),
            pltpu.VMEM((kept_total // 4, columns), BF16),
            pltpu.VMEM((key_total // lanes, 8, lanes), F32),
            pltpu.VMEM((n, 8, lanes), F32),
            pltpu.VMEM((8, lanes), F32),
            pltpu.VMEM((8, lanes), F32),
            dma((11,)),
            dma,
            dma((pairs,)), dma((pairs,)),
            dma((pairs,)), dma((pairs,)),
            dma((n,)), dma((n,)),
            dma((n,)), dma((n,)),
            dma((n,)), dma((n,)),
            dma((chunks, 1 + pairs + quads)), dma((chunks, 1 + pairs + quads)),
            dma((n,)), dma((n,)),
            dma, dma,
        ],
        compiler_params=pltpu.CompilerParams(
            collective_id=0, has_side_effects=True, vmem_limit_bytes=56 * 2 ** 20
        ),
    )(
        queries, keys, values, hidden, norm_gain.reshape(1, width),
        retained_lists.reshape(1, rows), counts.reshape(1, n), affine_matrix,
        affine_offset_vector,
    )
    context, col_scores, projected = pl.pallas_call(
        hand_over,
        out_shape=(
            jax.ShapeDtypeStruct(context.shape, F32),
            jax.ShapeDtypeStruct(col_scores.shape, F32),
            jax.ShapeDtypeStruct(projected.shape, F32),
        ),
        in_specs=[vmem, vmem, vmem],
        out_specs=(vmem, vmem, vmem),
        compiler_params=pltpu.CompilerParams(vmem_limit_bytes=8 * 2 ** 20),
    )(context, col_scores, projected)
    return (context, col_scores.reshape(rows), projected)


def solution(mesh):
    in_specs = (
        P(("grp", "seq"), "ten"),
        P(("grp", "seq"), "ten"),
        P(("grp", "seq"), "ten"),
        P(("grp", "seq"), None),
        P(),
        P(("grp", "seq")),
        P("grp"),
        P("seq", "ten"),
        P("ten"),
    )
    out_specs = (P(("grp", "seq"), "ten"), P(("grp", "seq")), P(("grp", "seq"), "ten"))
    return jax.shard_map(
        functools.partial(shards, mesh.shape["seq"]),
        mesh=mesh, in_specs=in_specs, out_specs=out_specs, check_vma=False,
    )
```

```python
import functools
import math

import jax
import jax.numpy as jnp
from jax import lax
from jax.experimental import pallas as pl
from jax.experimental.pallas import tpu as pltpu
from jax.sharding import PartitionSpec as P

HEAD_SIZE = 128
QUERY_HEADS = 32
F32 = jnp.float32
BF16 = jnp.bfloat16


def remote(src, dst, send_sem, recv_sem, where):
    return pltpu.make_async_remote_copy(
        src_ref=src,
        dst_ref=dst,
        send_sem=send_sem,
        recv_sem=recv_sem,
        device_id=where,
        device_id_type=pl.DeviceIdType.MESH,
    )


def kernel(
    n, plan,
    q_hbm, k_hbm, v_hbm, h_hbm, gain_hbm, list_hbm, count_hbm, a_hbm, bias_hbm,
    ctx_ref, col_ref, out_ref,
    q_ref, h_ref, gain_ref, list_ref, count_ref, bias_ref, a_ref,
    kvbuf, s_ref, e_ref, raw_ref, norm_ref, note_send, note_recv, g_ref, comp_ref,
    s1_ref, r1_ref, own_ref, s2_ref, r2_ref, s3_ref, r3_ref,
    c_send, c_recv, ct_send, ct_recv,
    in_sem, a_sem, kz_ssem, kz_rsem, ky_ssem, ky_rsem, sv_ssem, sv_rsem, nt_ssem, nt_rsem,
    fw_ssem, fw_rsem, rs_ssem, rs_rsem, c_ssem, c_rsem, ct_ssem, ct_rsem,
):
    me = lax.axis_index("seq")
    ten = lax.axis_index("ten")
    sibling = {"ten": 1 - ten}
    rows = q_ref.shape[0]
    key_total = n * rows
    kv_heads = k_hbm.shape[1] // HEAD_SIZE
    group = q_ref.shape[1] // k_hbm.shape[1]
    width = h_ref.shape[1]
    half = width // n // 2
    out_rows = out_ref.shape[0]
    pairs = n // 2
    quads = pairs // 2
    quad_rows = quads * out_rows
    parity = lax.rem(me, 2)
    pair = lax.div(me, 2)
    partner = {"seq": me + 1 - 2 * parity}
    pair_parity = lax.rem(pair, 2)
    other_pair = pair + 1 - 2 * pair_parity
    other = {"seq": 2 * other_pair + parity}

    def block_columns(owner, side):
        return pl.ds(pl.multiple_of(owner * (2 * half) + side * half, 128), half)

    h_copy = pltpu.make_async_copy(h_hbm, h_ref, in_sem.at[0])
    h_copy.start()
    barrier = pltpu.get_barrier_semaphore()
    for d in range(1, n):
        pl.semaphore_signal(
            barrier, inc=1, device_id={"seq": lax.rem(me + d, n)},
            device_id_type=pl.DeviceIdType.MESH,
        )
    pl.semaphore_signal(
        barrier, inc=1, device_id=sibling, device_id_type=pl.DeviceIdType.MESH
    )
    kv_copies = [
        pltpu.make_async_copy(k_hbm, kvbuf.at[me, 0], in_sem.at[1]),
        pltpu.make_async_copy(v_hbm, kvbuf.at[me, 1], in_sem.at[2]),
    ]
    note_copies = [
        pltpu.make_async_copy(list_hbm, list_ref, in_sem.at[3]),
        pltpu.make_async_copy(count_hbm, count_ref, in_sem.at[4]),
    ]
    own_copies = [
        pltpu.make_async_copy(
            h_hbm.at[:, block_columns(me, side)], raw_ref.at[side, 0], in_sem.at[5 + side]
        )
        for side in range(2)
    ] + [
        pltpu.make_async_copy(
            gain_hbm.at[:, block_columns(me, side)], gain_ref.at[side], in_sem.at[7 + side]
        )
        for side in range(2)
    ]
    late_copies = [
        pltpu.make_async_copy(q_hbm, q_ref, in_sem.at[9]),
        pltpu.make_async_copy(bias_hbm, bias_ref, in_sem.at[10]),
    ]
    a_copy = pltpu.make_async_copy(a_hbm, a_ref, a_sem)
    for copy in kv_copies + note_copies + own_copies:
        copy.start()
    pl.semaphore_wait(barrier, n)

    def chain(age):
        block = kvbuf.at[2 * (pair - age) + parity]
        target = {"seq": me + 2}
        return remote(block, block, kz_ssem.at[age], kz_rsem.at[age + 1], target)

    def chain_in(age):
        block = kvbuf.at[2 * (pair - age) + parity]
        return remote(block, block, kz_ssem.at[age - 1], kz_rsem.at[age], partner)

    def across(age):
        block = kvbuf.at[2 * (pair - age) + parity]
        return remote(block, block, ky_ssem.at[age], ky_rsem.at[age], partner)

    def across_in(age):
        block = kvbuf.at[2 * (pair - age) + 1 - parity]
        return remote(block, block, ky_ssem.at[age], ky_rsem.at[age], partner)

    def relay(age):
        @pl.when(pair >= age)
        def _():
            chain_in(age).wait_recv()

            @pl.when(pair + 1 < pairs)
            def _():
                if age + 1 < pairs:
                    chain(age).start()

            across(age).start()

    def raw_copy(d, target):
        return remote(
            (h_hbm if d in order[:first_sends] else h_ref).at[:, block_columns(target, ten)],
            raw_ref.at[ten, d],
            sv_ssem.at[d], sv_rsem.at[d], {"seq": target},
        )

    def note_copy(d, target):
        return remote(
            note_send, note_recv.at[d], nt_ssem.at[d], nt_rsem.at[d], {"seq": target}
        )

    def forward(d, side):
        block = raw_ref.at[side, d]
        return remote(block, block, fw_ssem.at[d], fw_rsem.at[d], sibling)

    order = sorted(range(1, n), key=lambda d: abs(2 * d - n))
    first_sends = 2
    lag = 3
    for copy in kv_copies:
        copy.wait()

    @pl.when(pair + 1 < pairs)
    def _():
        chain(0).start()

    for d in order[:first_sends]:
        raw_copy(d, lax.rem(me + d, n)).start()

    @pl.when(parity == 0)
    def _():
        across(0).start()

    lane = lax.broadcasted_iota(jnp.int32, (rows, rows), 1)
    line = lax.broadcasted_iota(jnp.int32, (rows, rows), 0)
    for copy in note_copies:
        copy.wait()
    shard_at = lax.broadcasted_iota(jnp.int32, (1, n), 1)
    opening = jnp.sum(
        jnp.where(shard_at < me, count_ref[...], 0), axis=1, keepdims=True
    )
    kept = jnp.sum(jnp.where(lane == line, list_ref[...], 0), axis=1, keepdims=True)
    place = jnp.sum(
        jnp.where(kept == lane, opening + line + 1, 0), axis=0, keepdims=True
    ) - 1
    h_copy.wait()
    square = jnp.zeros((rows, 1), F32)
    step = math.gcd(width, 1024)
    for c in range(width // step):
        x = h_ref[:, c * step:(c + 1) * step].astype(F32)
        square = square + jnp.sum(x * x, axis=1, keepdims=True)
    rescale = lax.rsqrt(square / width + 1e-06)
    note_send[...] = jnp.zeros_like(note_send)
    note_send[0:1, :rows] = jnp.sum(
        jnp.where(lane == line, rescale, 0.0), axis=0, keepdims=True
    )
    note_send[1:2, :rows] = place.astype(F32)
    note_recv[0] = note_send[...]
    for d in order:
        note_copy(d, lax.rem(me + d, n)).start()
    relay(1)
    for d in order[first_sends:]:
        raw_copy(d, lax.rem(me + d, n)).start()
    a_copy.start()
    for copy in late_copies:
        copy.start()

    def clear(j, carry):
        kvbuf[j] = jnp.zeros_like(kvbuf[j])
        return carry

    lax.fori_loop(me + 1, n, clear, 0)
    for copy in own_copies:
        copy.wait()

    def normalise(d):
        scale = jnp.sum(
            jnp.where(lane == line, note_recv[d, 0:1, :rows], 0.0), axis=1, keepdims=True
        )
        for side in range(2):
            x = raw_ref[side, d].astype(F32) * scale * gain_ref[side]
            norm_ref[side, d * rows:(d + 1) * rows, :] = x.astype(BF16)

    def settle(d):
        forward(d, 1 - ten).wait_recv()
        normalise(d)

    normalise(0)
    for at, d in enumerate(order):
        raw_copy(d, me).wait_recv()
        forward(d, ten).start()
        if at % 2 == 0 and 0 < at < n - 2:
            relay(at // 2 + 1)
        note_copy(d, me).wait_recv()
        if at >= lag:
            settle(order[at - lag])

    places = jnp.concatenate(
        [note_recv[d, 1:2, :rows] for d in range(n)], axis=1
    ).astype(jnp.int32)
    row_at = lax.broadcasted_iota(jnp.int32, (out_rows, key_total), 0)
    for side in range(2):
        side_parity = 1 - parity if side == 0 else parity
        for d in range(pairs):
            origin = other_pair if d < quads else pair
            base = (2 * lax.rem(origin + 2 * (d % quads), pairs) + side_parity) * out_rows
            first = (side * pairs + d) * out_rows
            g_ref[first:first + out_rows, :] = (
                (row_at + base == places).astype(F32).astype(BF16)
            )
    for d in order[-lag:]:
        settle(d)
    for side in range(2):
        comp_ref[:, side * half:(side + 1) * half] = jnp.dot(
            g_ref[...], norm_ref[side], preferred_element_type=F32
        ).astype(BF16)
    a_copy.wait()

    half_rows = 2 * quad_rows

    def rs_copy(c, slot, src, dst, target):
        return remote(src, dst, rs_ssem.at[c, slot], rs_rsem.at[c, slot], target)

    def lines(ref, c, first, count):
        start, size = plan[c][1:]
        return ref.at[first:first + count, start:start + size]

    def step_one(c):
        target = other if plan[c][0] == "W" else partner
        return rs_copy(
            c, 0, lines(s1_ref, c, 0, half_rows), lines(r1_ref, c, 0, half_rows), target
        )

    def step_two(c):
        kind = plan[c][0]
        if kind == "Y":
            return [rs_copy(
                c, 1, lines(s2_ref, c, 0, quad_rows), lines(r2_ref, c, 0, quad_rows), other
            )]
        copies = []
        if kind == "D":
            for j in sorted(range(pairs), key=lambda j: j % quads, reverse=True):
                if j != quads:
                    base = other_pair if j < quads else pair
                    target = {"seq": 2 * lax.rem(base + 2 * (j % quads), pairs) + parity}
                    copies.append(rs_copy(
                        c, 1 + j, lines(s2_ref, c, j * out_rows, out_rows),
                        lines(r2_ref, c, j * out_rows, out_rows), target,
                    ))
        else:
            for d in range(1, quads):
                target = {"seq": 2 * lax.rem(pair + 2 * d, pairs) + parity}
                copies.append(rs_copy(
                    c, 1 + d, lines(s2_ref, c, 2 * d * out_rows, 2 * out_rows),
                    lines(r2_ref, c, 2 * d * out_rows, 2 * out_rows), target,
                ))
        return copies

    def step_three(c):
        kind = plan[c][0]
        if kind == "D":
            return []
        if kind == "W":
            return [rs_copy(
                c, 1 + pairs, lines(s3_ref, c, 0, out_rows), lines(r3_ref, c, 0, out_rows),
                partner,
            )]
        return [
            rs_copy(
                c, 1 + pairs + d, lines(s3_ref, c, d * out_rows, out_rows),
                lines(r3_ref, c, d * out_rows, out_rows),
                {"seq": 2 * lax.rem(pair + 2 * d, pairs) + parity},
            )
            for d in range(1, quads)
        ]

    def columns_of(c):
        return slice(plan[c][1], plan[c][1] + plan[c][2])

    def after_one(c):
        kind, cols = plan[c][0], columns_of(c)
        step_one(c).wait_recv()
        if kind == "Y":
            s2_ref[:quad_rows, cols] = (
                own_ref[:quad_rows, cols] + r1_ref[:quad_rows, cols].astype(F32)
            ).astype(BF16)
        elif kind == "D":
            for j in range(pairs):
                if j != quads:
                    part = slice(j * out_rows, (j + 1) * out_rows)
                    s2_ref[part, cols] = (
                        own_ref[part, cols] + r1_ref[part, cols].astype(F32)
                    ).astype(BF16)
        else:
            for d in range(1, quads):
                for q in range(2):
                    part = slice(q * quad_rows + d * out_rows, q * quad_rows + (d + 1) * out_rows)
                    place_at = (2 * d + q) * out_rows
                    s2_ref[place_at:place_at + out_rows, cols] = (
                        own_ref[part, cols] + r1_ref[part, cols].astype(F32)
                    ).astype(BF16)
        for copy in step_two(c):
            copy.start()

    def after_two(c):
        kind, cols = plan[c][0], columns_of(c)
        for copy in step_two(c):
            copy.wait_recv()
        if kind == "Y":
            for d in range(1, quads):
                part = slice(quad_rows + d * out_rows, quad_rows + (d + 1) * out_rows)
                s3_ref[d * out_rows:(d + 1) * out_rows, cols] = (
                    own_ref[part, cols]
                    + r1_ref[part, cols].astype(F32)
                    + r2_ref[d * out_rows:(d + 1) * out_rows, cols].astype(F32)
                ).astype(BF16)
        elif kind == "W":
            total = own_ref[:out_rows, cols] + r1_ref[:out_rows, cols].astype(F32)
            for d in range(1, quads):
                first = 2 * d * out_rows
                total = total + r2_ref[first:first + out_rows, cols].astype(F32)
            s3_ref[:out_rows, cols] = total.astype(BF16)
        for copy in step_three(c):
            copy.start()

    def finish(c):
        kind, cols = plan[c][0], columns_of(c)
        for copy in step_three(c):
            copy.wait_recv()
        mine = slice(quad_rows, quad_rows + out_rows)
        total = own_ref[mine, cols] + r1_ref[mine, cols].astype(F32)
        if kind == "Y":
            total = total + r2_ref[:out_rows, cols].astype(F32)
            for d in range(1, quads):
                total = total + r3_ref[d * out_rows:(d + 1) * out_rows, cols].astype(F32)
        elif kind == "D":
            for j in range(pairs):
                if j != quads:
                    total = total + r2_ref[j * out_rows:(j + 1) * out_rows, cols].astype(F32)
        else:
            for d in range(1, quads):
                first = (2 * d + 1) * out_rows
                total = total + r2_ref[first:first + out_rows, cols].astype(F32)
            total = total + r3_ref[:out_rows, cols].astype(F32)
        out_ref[:, cols] = total + bias_ref[cols].reshape(1, plan[c][2])

    for c in range(len(plan)):
        cols = columns_of(c)
        part = jnp.dot(comp_ref[...], a_ref[:, cols], preferred_element_type=F32)
        quarters = [part[i * quad_rows:(i + 1) * quad_rows] for i in range(4)]
        away, stay = ((0, 2), (1, 3)) if plan[c][0] == "W" else ((0, 1), (2, 3))
        for i in range(2):
            s1_ref[i * quad_rows:(i + 1) * quad_rows, cols] = quarters[away[i]].astype(BF16)
        step_one(c).start()
        for i in range(2):
            own_ref[i * quad_rows:(i + 1) * quad_rows, cols] = quarters[stay[i]]

    def await_keys():
        @pl.when(parity == 1)
        def _():
            across_in(0).wait_recv()

        for age in range(1, pairs):

            @pl.when(pair >= age)
            def _():
                across_in(age).wait_recv()

        for copy in late_copies:
            copy.wait()

    def attend(h, columns_total):
        key_pos = lax.broadcasted_iota(jnp.int32, (rows, key_total), 1)
        query_pos = me * rows + lax.broadcasted_iota(jnp.int32, (rows, key_total), 0)
        allowed = key_pos <= query_pos
        heads = slice(h * HEAD_SIZE, (h + 1) * HEAD_SIZE)
        query = jnp.concatenate(
            [
                q_ref[:, (h * group + a) * HEAD_SIZE:(h * group + a + 1) * HEAD_SIZE]
                for a in range(group)
            ],
            axis=0,
        )
        key = kvbuf[:, 0, :, heads].reshape(key_total, HEAD_SIZE)
        value = kvbuf[:, 1, :, heads].reshape(key_total, HEAD_SIZE)
        s_ref[...] = lax.dot_general(
            query, key, (((1,), (1,)), ((), ())), preferred_element_type=F32
        )
        inverses = []
        for a in range(group):
            part = slice(a * rows, (a + 1) * rows)
            scores = jnp.where(allowed, s_ref[part, :] * HEAD_SIZE ** (-0.5), -1e30)
            largest = jnp.max(scores, axis=1, keepdims=True)
            weights = jnp.where(allowed, jnp.exp(scores - largest), 0.0)
            e_ref[part, :] = weights.astype(BF16)
            inverse = 1.0 / jnp.sum(weights, axis=1, keepdims=True)
            inverses.append(inverse)
            columns_total = columns_total + jnp.sum(
                (weights * inverse).reshape(rows // 8, 8, key_total), axis=0
            )
        mixed = jnp.dot(e_ref[...], value, preferred_element_type=F32)
        for a in range(group):
            place_at = (h * group + a) * HEAD_SIZE
            ctx_ref[:, place_at:place_at + HEAD_SIZE] = (
                mixed[a * rows:(a + 1) * rows] * inverses[a]
            )
        return columns_total

    lanes = c_send.shape[2]
    per = lanes // rows

    def col_copy(d, owner, target):
        return remote(
            c_send.at[lax.div(owner, per)], c_recv.at[d], c_ssem.at[d], c_rsem.at[d],
            {"seq": target},
        )

    def send_columns(columns_total):
        for b in range(n // per):
            c_send[b] = columns_total[:, b * lanes:(b + 1) * lanes]
        for d in range(1, n):

            @pl.when(me - d >= 0)
            def _():
                col_copy(d, me - d, me - d).start()

    ct = remote(ct_send, ct_recv, ct_ssem, ct_rsem, sibling)

    def sum_columns():
        mine = c_send[lax.div(me, per)]
        for d in range(1, n):
            c_recv_valid = me + d < n

            @pl.when(c_recv_valid)
            def _():
                col_copy(d, me, me).wait_recv()

            @pl.when(jnp.logical_not(c_recv_valid))
            def _():
                c_recv[d] = jnp.zeros_like(c_recv[d])

            mine = mine + c_recv[d]
        ct_send[...] = mine
        ct.start()

    state = {"columns": jnp.zeros((8, key_total), F32)}

    def attention(h):
        if h == 0:
            await_keys()
        state["columns"] = attend(h, state["columns"])
        if h == kv_heads - 1:
            send_columns(state["columns"])

    after_one(0)
    after_one(1)
    after_one(2)
    attention(0)
    after_one(3)
    after_two(0)
    for h in range(1, kv_heads):
        attention(h)
    after_two(1)
    after_one(4)
    after_two(2)
    after_two(3)
    after_one(5)
    sum_columns()
    finish(1)
    after_one(6)
    finish(0)
    finish(2)
    after_two(4)
    finish(3)
    after_two(5)
    finish(5)
    after_two(6)
    finish(6)
    finish(4)

    ct.wait()
    both = jnp.sum(ct_send[...] + ct_recv[...], axis=0, keepdims=True) / QUERY_HEADS
    turn = lax.rem(me, per)
    picked = both[:, :rows]
    for b in range(1, per):
        picked = jnp.where(turn == b, both[:, b * rows:(b + 1) * rows], picked)
    col_ref[...] = picked

    for d in range(1, n):

        @pl.when(me - d >= 0)
        def _():
            col_copy(d, me - d, me - d).wait_send()

        raw_copy(d, lax.rem(me + d, n)).wait_send()
        note_copy(d, lax.rem(me + d, n)).wait_send()
        forward(d, ten).wait_send()

    @pl.when(parity == 0)
    def _():
        across(0).wait_send()

    @pl.when(pair + 1 < pairs)
    def _():
        chain(0).wait_send()

    for age in range(1, pairs):

        @pl.when(pair >= age)
        def _():
            across(age).wait_send()

        if age + 1 < pairs:

            @pl.when((pair >= age) & (pair + 1 < pairs))
            def _():
                chain(age).wait_send()

    for c in range(len(plan)):
        for copy in [step_one(c)] + step_two(c) + step_three(c):
            copy.wait_send()


def hand_over(context, scores, projected, context_out, scores_out, projected_out):
    context_out[...] = context[...]
    scores_out[...] = scores[...]
    projected_out[...] = projected[...]


def shards(
    n, queries, keys, values, hidden, norm_gain, retained_lists, counts, affine_matrix,
    affine_offset_vector,
):
    rows, query_width = queries.shape
    width = hidden.shape[1]
    depth, columns = affine_matrix.shape
    kv_width = keys.shape[1]
    group = query_width // kv_width
    half = width // n // 2
    out_rows = rows // 2
    kept_total = n * out_rows
    pairs = n // 2
    quads = n // 4
    lanes = max(128, rows)
    key_total = n * rows
    plan, start = [], 0
    unit = columns // 20
    for kind, share in (("W", 3), ("Y", 3), ("W", 2), ("Y", 4), ("Y", 4), ("D", 3), ("D", 1)):
        plan.append((kind, start, share * unit))
        start += share * unit
    chunks = len(plan)
    vmem = pl.BlockSpec(memory_space=pltpu.VMEM)
    hbm = pl.BlockSpec(memory_space=pltpu.HBM)
    dma = pltpu.SemaphoreType.DMA
    context, col_scores, projected = pl.pallas_call(
        functools.partial(kernel, n, tuple(plan)),
        out_shape=(
            pltpu.VMEM((rows, query_width), F32),
            pltpu.VMEM((1, rows), F32),
            pltpu.VMEM((out_rows, columns), F32),
        ),
        in_specs=[hbm] * 9,
        out_specs=(vmem, vmem, vmem),
        scratch_shapes=[
            pltpu.VMEM((rows, query_width), BF16),
            pltpu.VMEM((rows, width), BF16),
            pltpu.VMEM((2, 1, half), F32),
            pltpu.VMEM((1, rows), jnp.int32),
            pltpu.VMEM((1, n), jnp.int32),
            pltpu.VMEM((columns,), F32),
            pltpu.VMEM((depth, columns), BF16),
            pltpu.VMEM((n, 2, rows, kv_width), BF16),
            pltpu.VMEM((group * rows, key_total), F32),
            pltpu.VMEM((group * rows, key_total), BF16),
            pltpu.VMEM((2, n, rows, half), BF16),
            pltpu.VMEM((2, key_total, half), BF16),
            pltpu.VMEM((8, lanes), F32),
            pltpu.VMEM((n, 8, lanes), F32),
            pltpu.VMEM((kept_total, key_total), BF16),
            pltpu.VMEM((kept_total, 2 * half), BF16),
            pltpu.VMEM((kept_total // 2, columns), BF16),
            pltpu.VMEM((kept_total // 2, columns), BF16),
            pltpu.VMEM((kept_total // 2, columns), F32),
            pltpu.VMEM((kept_total // 2, columns), BF16),
            pltpu.VMEM((kept_total // 2, columns), BF16),
            pltpu.VMEM((kept_total // 4, columns), BF16),
            pltpu.VMEM((kept_total // 4, columns), BF16),
            pltpu.VMEM((key_total // lanes, 8, lanes), F32),
            pltpu.VMEM((n, 8, lanes), F32),
            pltpu.VMEM((8, lanes), F32),
            pltpu.VMEM((8, lanes), F32),
            dma((11,)),
            dma,
            dma((pairs,)), dma((pairs,)),
            dma((pairs,)), dma((pairs,)),
            dma((n,)), dma((n,)),
            dma((n,)), dma((n,)),
            dma((n,)), dma((n,)),
            dma((chunks, 1 + pairs + quads)), dma((chunks, 1 + pairs + quads)),
            dma((n,)), dma((n,)),
            dma, dma,
        ],
        compiler_params=pltpu.CompilerParams(
            collective_id=0, has_side_effects=True, vmem_limit_bytes=56 * 2 ** 20
        ),
    )(
        queries, keys, values, hidden, norm_gain.reshape(1, width),
        retained_lists.reshape(1, rows), counts.reshape(1, n), affine_matrix,
        affine_offset_vector,
    )
    context, col_scores, projected = pl.pallas_call(
        hand_over,
        out_shape=(
            jax.ShapeDtypeStruct(context.shape, F32),
            jax.ShapeDtypeStruct(col_scores.shape, F32),
            jax.ShapeDtypeStruct(projected.shape, F32),
        ),
        in_specs=[vmem, vmem, vmem],
        out_specs=(vmem, vmem, vmem),
        compiler_params=pltpu.CompilerParams(vmem_limit_bytes=8 * 2 ** 20),
    )(context, col_scores, projected)
    return (context, col_scores.reshape(rows), projected)


def solution(mesh):
    in_specs = (
        P(("grp", "seq"), "ten"),
        P(("grp", "seq"), "ten"),
        P(("grp", "seq"), "ten"),
        P(("grp", "seq"), None),
        P(),
        P(("grp", "seq")),
        P("grp"),
        P("seq", "ten"),
        P("ten"),
    )
    out_specs = (P(("grp", "seq"), "ten"), P(("grp", "seq")), P(("grp", "seq"), "ten"))
    return jax.shard_map(
        functools.partial(shards, mesh.shape["seq"]),
        mesh=mesh, in_specs=in_specs, out_specs=out_specs, check_vma=False,
    )
```

```python
import functools
import math

import jax
import jax.numpy as jnp
from jax import lax
from jax.experimental import pallas as pl
from jax.experimental.pallas import tpu as pltpu
from jax.sharding import PartitionSpec as P

HEAD_SIZE = 128
QUERY_HEADS = 32
F32 = jnp.float32
BF16 = jnp.bfloat16


def remote(src, dst, send_sem, recv_sem, where):
    return pltpu.make_async_remote_copy(
        src_ref=src,
        dst_ref=dst,
        send_sem=send_sem,
        recv_sem=recv_sem,
        device_id=where,
        device_id_type=pl.DeviceIdType.MESH,
    )


def kernel(
    n, plan,
    q_hbm, k_hbm, v_hbm, h_hbm, gain_hbm, list_hbm, count_hbm, a_hbm, bias_hbm,
    ctx_ref, col_ref, out_ref,
    q_ref, h_ref, gain_ref, list_ref, count_ref, bias_ref, a_ref,
    kvbuf, s_ref, e_ref, raw_ref, norm_ref, note_send, note_recv, g_ref, comp_ref,
    s1_ref, r1_ref, own_ref, s2_ref, r2_ref, s3_ref, r3_ref,
    c_send, c_recv, ct_send, ct_recv,
    in_sem, a_sem, kz_ssem, kz_rsem, ky_ssem, ky_rsem, sv_ssem, sv_rsem, nt_ssem, nt_rsem,
    fw_ssem, fw_rsem, rs_ssem, rs_rsem, c_ssem, c_rsem, ct_ssem, ct_rsem,
):
    me = lax.axis_index("seq")
    ten = lax.axis_index("ten")
    sibling = {"ten": 1 - ten}
    rows = q_ref.shape[0]
    key_total = n * rows
    kv_heads = k_hbm.shape[1] // HEAD_SIZE
    group = q_ref.shape[1] // k_hbm.shape[1]
    width = h_ref.shape[1]
    half = width // n // 2
    out_rows = out_ref.shape[0]
    pairs = n // 2
    quads = pairs // 2
    quad_rows = quads * out_rows
    parity = lax.rem(me, 2)
    pair = lax.div(me, 2)
    partner = {"seq": me + 1 - 2 * parity}
    pair_parity = lax.rem(pair, 2)
    other_pair = pair + 1 - 2 * pair_parity
    other = {"seq": 2 * other_pair + parity}

    def block_columns(owner, side):
        return pl.ds(pl.multiple_of(owner * (2 * half) + side * half, 128), half)

    h_copy = pltpu.make_async_copy(h_hbm, h_ref, in_sem.at[0])
    h_copy.start()
    barrier = pltpu.get_barrier_semaphore()
    for d in range(1, n):
        pl.semaphore_signal(
            barrier, inc=1, device_id={"seq": lax.rem(me + d, n)},
            device_id_type=pl.DeviceIdType.MESH,
        )
    pl.semaphore_signal(
        barrier, inc=1, device_id=sibling, device_id_type=pl.DeviceIdType.MESH
    )
    kv_copies = [
        pltpu.make_async_copy(k_hbm, kvbuf.at[me, 0], in_sem.at[1]),
        pltpu.make_async_copy(v_hbm, kvbuf.at[me, 1], in_sem.at[2]),
    ]
    note_copies = [
        pltpu.make_async_copy(list_hbm, list_ref, in_sem.at[3]),
        pltpu.make_async_copy(count_hbm, count_ref, in_sem.at[4]),
    ]
    own_copies = [
        pltpu.make_async_copy(
            h_hbm.at[:, block_columns(me, side)], raw_ref.at[side, 0], in_sem.at[5 + side]
        )
        for side in range(2)
    ] + [
        pltpu.make_async_copy(
            gain_hbm.at[:, block_columns(me, side)], gain_ref.at[side], in_sem.at[7 + side]
        )
        for side in range(2)
    ]
    late_copies = [
        pltpu.make_async_copy(q_hbm, q_ref, in_sem.at[9]),
        pltpu.make_async_copy(bias_hbm, bias_ref, in_sem.at[10]),
    ]
    a_copy = pltpu.make_async_copy(a_hbm, a_ref, a_sem)
    for copy in kv_copies + note_copies + own_copies:
        copy.start()
    pl.semaphore_wait(barrier, n)

    def chain(age):
        block = kvbuf.at[2 * (pair - age) + parity]
        target = {"seq": me + 2}
        return remote(block, block, kz_ssem.at[age], kz_rsem.at[age + 1], target)

    def chain_in(age):
        block = kvbuf.at[2 * (pair - age) + parity]
        return remote(block, block, kz_ssem.at[age - 1], kz_rsem.at[age], partner)

    def across(age):
        block = kvbuf.at[2 * (pair - age) + parity]
        return remote(block, block, ky_ssem.at[age], ky_rsem.at[age], partner)

    def across_in(age):
        block = kvbuf.at[2 * (pair - age) + 1 - parity]
        return remote(block, block, ky_ssem.at[age], ky_rsem.at[age], partner)

    def relay(age):
        @pl.when(pair >= age)
        def _():
            chain_in(age).wait_recv()

            @pl.when(pair + 1 < pairs)
            def _():
                if age + 1 < pairs:
                    chain(age).start()

            across(age).start()

    def raw_copy(d, target):
        return remote(
            (h_hbm if d in order[:first_sends] else h_ref).at[:, block_columns(target, ten)],
            raw_ref.at[ten, d],
            sv_ssem.at[d], sv_rsem.at[d], {"seq": target},
        )

    def note_copy(d, target):
        return remote(
            note_send, note_recv.at[d], nt_ssem.at[d], nt_rsem.at[d], {"seq": target}
        )

    def forward(d, side):
        block = raw_ref.at[side, d]
        return remote(block, block, fw_ssem.at[d], fw_rsem.at[d], sibling)

    order = sorted(range(1, n), key=lambda d: abs(2 * d - n))
    first_sends = 2
    lag = 3
    for copy in kv_copies:
        copy.wait()

    @pl.when(pair + 1 < pairs)
    def _():
        chain(0).start()

    for d in order[:first_sends]:
        raw_copy(d, lax.rem(me + d, n)).start()

    @pl.when(parity == 0)
    def _():
        across(0).start()

    lane = lax.broadcasted_iota(jnp.int32, (rows, rows), 1)
    line = lax.broadcasted_iota(jnp.int32, (rows, rows), 0)
    for copy in note_copies:
        copy.wait()
    shard_at = lax.broadcasted_iota(jnp.int32, (1, n), 1)
    opening = jnp.sum(
        jnp.where(shard_at < me, count_ref[...], 0), axis=1, keepdims=True
    )
    kept = jnp.sum(jnp.where(lane == line, list_ref[...], 0), axis=1, keepdims=True)
    place = jnp.sum(
        jnp.where(kept == lane, opening + line + 1, 0), axis=0, keepdims=True
    ) - 1
    h_copy.wait()
    square = jnp.zeros((rows, 1), F32)
    step = math.gcd(width, 1024)
    for c in range(width // step):
        x = h_ref[:, c * step:(c + 1) * step].astype(F32)
        square = square + jnp.sum(x * x, axis=1, keepdims=True)
    rescale = lax.rsqrt(square / width + 1e-06)
    note_send[...] = jnp.zeros_like(note_send)
    note_send[0:1, :rows] = jnp.sum(
        jnp.where(lane == line, rescale, 0.0), axis=0, keepdims=True
    )
    note_send[1:2, :rows] = place.astype(F32)
    note_recv[0] = note_send[...]
    for d in order:
        note_copy(d, lax.rem(me + d, n)).start()
    relay(1)
    for d in order[first_sends:]:
        raw_copy(d, lax.rem(me + d, n)).start()
    a_copy.start()
    for copy in late_copies:
        copy.start()

    def clear(j, carry):
        kvbuf[j] = jnp.zeros_like(kvbuf[j])
        return carry

    lax.fori_loop(me + 1, n, clear, 0)
    for copy in own_copies:
        copy.wait()

    def normalise(d):
        scale = jnp.sum(
            jnp.where(lane == line, note_recv[d, 0:1, :rows], 0.0), axis=1, keepdims=True
        )
        for side in range(2):
            x = raw_ref[side, d].astype(F32) * scale * gain_ref[side]
            norm_ref[side, d * rows:(d + 1) * rows, :] = x.astype(BF16)

    def settle(d):
        forward(d, 1 - ten).wait_recv()
        normalise(d)

    normalise(0)
    for at, d in enumerate(order):
        raw_copy(d, me).wait_recv()
        forward(d, ten).start()
        if at % 2 == 0 and 0 < at < n - 2:
            relay(at // 2 + 1)
        note_copy(d, me).wait_recv()
        if at >= lag:
            settle(order[at - lag])

    places = jnp.concatenate(
        [note_recv[d, 1:2, :rows] for d in range(n)], axis=1
    ).astype(jnp.int32)
    row_at = lax.broadcasted_iota(jnp.int32, (out_rows, key_total), 0)
    for side in range(2):
        side_parity = 1 - parity if side == 0 else parity
        for d in range(pairs):
            origin = other_pair if d < quads else pair
            base = (2 * lax.rem(origin + 2 * (d % quads), pairs) + side_parity) * out_rows
            first = (side * pairs + d) * out_rows
            g_ref[first:first + out_rows, :] = (
                (row_at + base == places).astype(F32).astype(BF16)
            )
    for d in order[-lag:]:
        settle(d)
    for side in range(2):
        comp_ref[:, side * half:(side + 1) * half] = jnp.dot(
            g_ref[...], norm_ref[side], preferred_element_type=F32
        ).astype(BF16)
    a_copy.wait()

    half_rows = 2 * quad_rows

    def rs_copy(c, slot, src, dst, target):
        return remote(src, dst, rs_ssem.at[c, slot], rs_rsem.at[c, slot], target)

    def lines(ref, c, first, count):
        start, size = plan[c][1:]
        return ref.at[first:first + count, start:start + size]

    def step_one(c):
        target = other if plan[c][0] == "W" else partner
        return rs_copy(
            c, 0, lines(s1_ref, c, 0, half_rows), lines(r1_ref, c, 0, half_rows), target
        )

    def step_two(c):
        kind = plan[c][0]
        if kind == "Y":
            return [rs_copy(
                c, 1, lines(s2_ref, c, 0, quad_rows), lines(r2_ref, c, 0, quad_rows), other
            )]
        copies = []
        if kind == "D":
            for j in sorted(range(pairs), key=lambda j: j % quads, reverse=True):
                if j != quads:
                    base = other_pair if j < quads else pair
                    target = {"seq": 2 * lax.rem(base + 2 * (j % quads), pairs) + parity}
                    copies.append(rs_copy(
                        c, 1 + j, lines(s2_ref, c, j * out_rows, out_rows),
                        lines(r2_ref, c, j * out_rows, out_rows), target,
                    ))
        else:
            for d in range(1, quads):
                target = {"seq": 2 * lax.rem(pair + 2 * d, pairs) + parity}
                copies.append(rs_copy(
                    c, 1 + d, lines(s2_ref, c, 2 * d * out_rows, 2 * out_rows),
                    lines(r2_ref, c, 2 * d * out_rows, 2 * out_rows), target,
                ))
        return copies

    def step_three(c):
        kind = plan[c][0]
        if kind == "D":
            return []
        if kind == "W":
            return [rs_copy(
                c, 1 + pairs, lines(s3_ref, c, 0, out_rows), lines(r3_ref, c, 0, out_rows),
                partner,
            )]
        return [
            rs_copy(
                c, 1 + pairs + d, lines(s3_ref, c, d * out_rows, out_rows),
                lines(r3_ref, c, d * out_rows, out_rows),
                {"seq": 2 * lax.rem(pair + 2 * d, pairs) + parity},
            )
            for d in range(1, quads)
        ]

    def columns_of(c):
        return slice(plan[c][1], plan[c][1] + plan[c][2])

    def after_one(c):
        kind, cols = plan[c][0], columns_of(c)
        step_one(c).wait_recv()
        if kind == "Y":
            s2_ref[:quad_rows, cols] = (
                own_ref[:quad_rows, cols] + r1_ref[:quad_rows, cols].astype(F32)
            ).astype(BF16)
        elif kind == "D":
            for j in range(pairs):
                if j != quads:
                    part = slice(j * out_rows, (j + 1) * out_rows)
                    s2_ref[part, cols] = (
                        own_ref[part, cols] + r1_ref[part, cols].astype(F32)
                    ).astype(BF16)
        else:
            for d in range(1, quads):
                for q in range(2):
                    part = slice(q * quad_rows + d * out_rows, q * quad_rows + (d + 1) * out_rows)
                    place_at = (2 * d + q) * out_rows
                    s2_ref[place_at:place_at + out_rows, cols] = (
                        own_ref[part, cols] + r1_ref[part, cols].astype(F32)
                    ).astype(BF16)
        for copy in step_two(c):
            copy.start()

    def after_two(c):
        kind, cols = plan[c][0], columns_of(c)
        for copy in step_two(c):
            copy.wait_recv()
        if kind == "Y":
            for d in range(1, quads):
                part = slice(quad_rows + d * out_rows, quad_rows + (d + 1) * out_rows)
                s3_ref[d * out_rows:(d + 1) * out_rows, cols] = (
                    own_ref[part, cols]
                    + r1_ref[part, cols].astype(F32)
                    + r2_ref[d * out_rows:(d + 1) * out_rows, cols].astype(F32)
                ).astype(BF16)
        elif kind == "W":
            total = own_ref[:out_rows, cols] + r1_ref[:out_rows, cols].astype(F32)
            for d in range(1, quads):
                first = 2 * d * out_rows
                total = total + r2_ref[first:first + out_rows, cols].astype(F32)
            s3_ref[:out_rows, cols] = total.astype(BF16)
        for copy in step_three(c):
            copy.start()

    def finish(c):
        kind, cols = plan[c][0], columns_of(c)
        for copy in step_three(c):
            copy.wait_recv()
        mine = slice(quad_rows, quad_rows + out_rows)
        total = own_ref[mine, cols] + r1_ref[mine, cols].astype(F32)
        if kind == "Y":
            total = total + r2_ref[:out_rows, cols].astype(F32)
            for d in range(1, quads):
                total = total + r3_ref[d * out_rows:(d + 1) * out_rows, cols].astype(F32)
        elif kind == "D":
            for j in range(pairs):
                if j != quads:
                    total = total + r2_ref[j * out_rows:(j + 1) * out_rows, cols].astype(F32)
        else:
            for d in range(1, quads):
                first = (2 * d + 1) * out_rows
                total = total + r2_ref[first:first + out_rows, cols].astype(F32)
            total = total + r3_ref[:out_rows, cols].astype(F32)
        out_ref[:, cols] = total + bias_ref[cols].reshape(1, plan[c][2])

    for c in range(len(plan)):
        cols = columns_of(c)
        part = jnp.dot(comp_ref[...], a_ref[:, cols], preferred_element_type=F32)
        quarters = [part[i * quad_rows:(i + 1) * quad_rows] for i in range(4)]
        away, stay = ((0, 2), (1, 3)) if plan[c][0] == "W" else ((0, 1), (2, 3))
        for i in range(2):
            s1_ref[i * quad_rows:(i + 1) * quad_rows, cols] = quarters[away[i]].astype(BF16)
        step_one(c).start()
        for i in range(2):
            own_ref[i * quad_rows:(i + 1) * quad_rows, cols] = quarters[stay[i]]

    def await_keys():
        @pl.when(parity == 1)
        def _():
            across_in(0).wait_recv()

        for age in range(1, pairs):

            @pl.when(pair >= age)
            def _():
                across_in(age).wait_recv()

        for copy in late_copies:
            copy.wait()

    def attend(h, columns_total):
        key_pos = lax.broadcasted_iota(jnp.int32, (rows, key_total), 1)
        query_pos = me * rows + lax.broadcasted_iota(jnp.int32, (rows, key_total), 0)
        allowed = key_pos <= query_pos
        heads = slice(h * HEAD_SIZE, (h + 1) * HEAD_SIZE)
        query = jnp.concatenate(
            [
                q_ref[:, (h * group + a) * HEAD_SIZE:(h * group + a + 1) * HEAD_SIZE]
                for a in range(group)
            ],
            axis=0,
        )
        key = kvbuf[:, 0, :, heads].reshape(key_total, HEAD_SIZE)
        value = kvbuf[:, 1, :, heads].reshape(key_total, HEAD_SIZE)
        s_ref[...] = lax.dot_general(
            query, key, (((1,), (1,)), ((), ())), preferred_element_type=F32
        )
        inverses = []
        for a in range(group):
            part = slice(a * rows, (a + 1) * rows)
            scores = jnp.where(allowed, s_ref[part, :] * HEAD_SIZE ** (-0.5), -1e30)
            largest = jnp.max(scores, axis=1, keepdims=True)
            weights = jnp.where(allowed, jnp.exp(scores - largest), 0.0)
            e_ref[part, :] = weights.astype(BF16)
            inverse = 1.0 / jnp.sum(weights, axis=1, keepdims=True)
            inverses.append(inverse)
            columns_total = columns_total + jnp.sum(
                (weights * inverse).reshape(rows // 8, 8, key_total), axis=0
            )
        mixed = jnp.dot(e_ref[...], value, preferred_element_type=F32)
        for a in range(group):
            place_at = (h * group + a) * HEAD_SIZE
            ctx_ref[:, place_at:place_at + HEAD_SIZE] = (
                mixed[a * rows:(a + 1) * rows] * inverses[a]
            )
        return columns_total

    lanes = c_send.shape[2]
    per = lanes // rows

    def col_copy(d, owner, target):
        return remote(
            c_send.at[lax.div(owner, per)], c_recv.at[d], c_ssem.at[d], c_rsem.at[d],
            {"seq": target},
        )

    def send_columns(columns_total):
        for b in range(n // per):
            c_send[b] = columns_total[:, b * lanes:(b + 1) * lanes]
        for d in range(1, n):

            @pl.when(me - d >= 0)
            def _():
                col_copy(d, me - d, me - d).start()

    ct = remote(ct_send, ct_recv, ct_ssem, ct_rsem, sibling)

    def sum_columns():
        mine = c_send[lax.div(me, per)]
        for d in range(1, n):
            c_recv_valid = me + d < n

            @pl.when(c_recv_valid)
            def _():
                col_copy(d, me, me).wait_recv()

            @pl.when(jnp.logical_not(c_recv_valid))
            def _():
                c_recv[d] = jnp.zeros_like(c_recv[d])

            mine = mine + c_recv[d]
        ct_send[...] = mine
        ct.start()

    state = {"columns": jnp.zeros((8, key_total), F32)}

    def attention(h):
        if h == 0:
            await_keys()
        state["columns"] = attend(h, state["columns"])
        if h == kv_heads - 1:
            send_columns(state["columns"])

    after_one(0)
    after_one(1)
    after_one(2)
    after_one(3)
    after_two(0)
    attention(0)
    after_two(1)
    for h in range(1, kv_heads):
        attention(h)
    after_one(4)
    after_two(2)
    after_two(3)
    after_one(5)
    finish(1)
    after_one(6)
    sum_columns()
    finish(0)
    finish(2)
    after_two(4)
    finish(3)
    after_two(5)
    finish(5)
    after_two(6)
    finish(6)
    finish(4)

    ct.wait()
    both = jnp.sum(ct_send[...] + ct_recv[...], axis=0, keepdims=True) / QUERY_HEADS
    turn = lax.rem(me, per)
    picked = both[:, :rows]
    for b in range(1, per):
        picked = jnp.where(turn == b, both[:, b * rows:(b + 1) * rows], picked)
    col_ref[...] = picked

    for d in range(1, n):

        @pl.when(me - d >= 0)
        def _():
            col_copy(d, me - d, me - d).wait_send()

        raw_copy(d, lax.rem(me + d, n)).wait_send()
        note_copy(d, lax.rem(me + d, n)).wait_send()
        forward(d, ten).wait_send()

    @pl.when(parity == 0)
    def _():
        across(0).wait_send()

    @pl.when(pair + 1 < pairs)
    def _():
        chain(0).wait_send()

    for age in range(1, pairs):

        @pl.when(pair >= age)
        def _():
            across(age).wait_send()

        if age + 1 < pairs:

            @pl.when((pair >= age) & (pair + 1 < pairs))
            def _():
                chain(age).wait_send()

    for c in range(len(plan)):
        for copy in [step_one(c)] + step_two(c) + step_three(c):
            copy.wait_send()


def hand_over(context, scores, projected, context_out, scores_out, projected_out):
    context_out[...] = context[...]
    scores_out[...] = scores[...]
    projected_out[...] = projected[...]


def shards(
    n, queries, keys, values, hidden, norm_gain, retained_lists, counts, affine_matrix,
    affine_offset_vector,
):
    rows, query_width = queries.shape
    width = hidden.shape[1]
    depth, columns = affine_matrix.shape
    kv_width = keys.shape[1]
    group = query_width // kv_width
    half = width // n // 2
    out_rows = rows // 2
    kept_total = n * out_rows
    pairs = n // 2
    quads = n // 4
    lanes = max(128, rows)
    key_total = n * rows
    plan, start = [], 0
    unit = columns // 20
    for kind, share in (("W", 3), ("Y", 3), ("W", 2), ("Y", 4), ("Y", 4), ("D", 3), ("D", 1)):
        plan.append((kind, start, share * unit))
        start += share * unit
    chunks = len(plan)
    vmem = pl.BlockSpec(memory_space=pltpu.VMEM)
    hbm = pl.BlockSpec(memory_space=pltpu.HBM)
    dma = pltpu.SemaphoreType.DMA
    context, col_scores, projected = pl.pallas_call(
        functools.partial(kernel, n, tuple(plan)),
        out_shape=(
            pltpu.VMEM((rows, query_width), F32),
            pltpu.VMEM((1, rows), F32),
            pltpu.VMEM((out_rows, columns), F32),
        ),
        in_specs=[hbm] * 9,
        out_specs=(vmem, vmem, vmem),
        scratch_shapes=[
            pltpu.VMEM((rows, query_width), BF16),
            pltpu.VMEM((rows, width), BF16),
            pltpu.VMEM((2, 1, half), F32),
            pltpu.VMEM((1, rows), jnp.int32),
            pltpu.VMEM((1, n), jnp.int32),
            pltpu.VMEM((columns,), F32),
            pltpu.VMEM((depth, columns), BF16),
            pltpu.VMEM((n, 2, rows, kv_width), BF16),
            pltpu.VMEM((group * rows, key_total), F32),
            pltpu.VMEM((group * rows, key_total), BF16),
            pltpu.VMEM((2, n, rows, half), BF16),
            pltpu.VMEM((2, key_total, half), BF16),
            pltpu.VMEM((8, lanes), F32),
            pltpu.VMEM((n, 8, lanes), F32),
            pltpu.VMEM((kept_total, key_total), BF16),
            pltpu.VMEM((kept_total, 2 * half), BF16),
            pltpu.VMEM((kept_total // 2, columns), BF16),
            pltpu.VMEM((kept_total // 2, columns), BF16),
            pltpu.VMEM((kept_total // 2, columns), F32),
            pltpu.VMEM((kept_total // 2, columns), BF16),
            pltpu.VMEM((kept_total // 2, columns), BF16),
            pltpu.VMEM((kept_total // 4, columns), BF16),
            pltpu.VMEM((kept_total // 4, columns), BF16),
            pltpu.VMEM((key_total // lanes, 8, lanes), F32),
            pltpu.VMEM((n, 8, lanes), F32),
            pltpu.VMEM((8, lanes), F32),
            pltpu.VMEM((8, lanes), F32),
            dma((11,)),
            dma,
            dma((pairs,)), dma((pairs,)),
            dma((pairs,)), dma((pairs,)),
            dma((n,)), dma((n,)),
            dma((n,)), dma((n,)),
            dma((n,)), dma((n,)),
            dma((chunks, 1 + pairs + quads)), dma((chunks, 1 + pairs + quads)),
            dma((n,)), dma((n,)),
            dma, dma,
        ],
        compiler_params=pltpu.CompilerParams(
            collective_id=0, has_side_effects=True, vmem_limit_bytes=56 * 2 ** 20
        ),
    )(
        queries, keys, values, hidden, norm_gain.reshape(1, width),
        retained_lists.reshape(1, rows), counts.reshape(1, n), affine_matrix,
        affine_offset_vector,
    )
    context, col_scores, projected = pl.pallas_call(
        hand_over,
        out_shape=(
            jax.ShapeDtypeStruct(context.shape, F32),
            jax.ShapeDtypeStruct(col_scores.shape, F32),
            jax.ShapeDtypeStruct(projected.shape, F32),
        ),
        in_specs=[vmem, vmem, vmem],
        out_specs=(vmem, vmem, vmem),
        compiler_params=pltpu.CompilerParams(vmem_limit_bytes=8 * 2 ** 20),
    )(context, col_scores, projected)
    return (context, col_scores.reshape(rows), projected)


def solution(mesh):
    in_specs = (
        P(("grp", "seq"), "ten"),
        P(("grp", "seq"), "ten"),
        P(("grp", "seq"), "ten"),
        P(("grp", "seq"), None),
        P(),
        P(("grp", "seq")),
        P("grp"),
        P("seq", "ten"),
        P("ten"),
    )
    out_specs = (P(("grp", "seq"), "ten"), P(("grp", "seq")), P(("grp", "seq"), "ten"))
    return jax.shard_map(
        functools.partial(shards, mesh.shape["seq"]),
        mesh=mesh, in_specs=in_specs, out_specs=out_specs, check_vma=False,
    )
```
